256 devices in a mesh: sub: 4 (over y), row: 4 (over x_lo, core), col: 16 (over z, x_hi).
Axes of the slice: x: 4 (x_hi: 2, x_lo: 2; x = x_hi * 2 + x_lo), y: 4, z: 8, core: 2. Of those that a mesh axis runs over, the one named last changes fastest.
Arguments:
- pressure_rhs: float32 [3, 4, 4096, 128], P(None, 'sub', 'col'), may hold values from -6 to 6
- diag_inverse: float32 [4, 4096, 7, 4096], P('sub', 'row', None, 'col'), as said below
- factor_blocks: float32 [3, 4, 2048, 4096], P(None, 'sub', 'col', 'row'), may hold values from -0.09375 to 0.09375
- row_lists: int32 [3, 4, 2048], P(None, 'sub', 'col'), may hold values from 0 to 16383, as said below
Outputs:
- solution: float32 [3, 4, 4096, 128], P(None, 'sub', 'col')
The draws below stay inside these ranges and needn't reach their ends.
Inputs may be any that keep to these rules, and one draw needn't show every extreme that they name: `diag_inverse`: in slot 2^l - 1 + q the block of row panel s is zero where q > s mod 2^l, and lower triangular with diagonal entries between 0.5 and 2 where q = s mod 2^l. row_lists[t, s, k] = q * 4096 + 2 k + e with e 0 or 1 and q below 2^m, m the upper level of pair t; entry 0 of every list is 0 and entry 2047 is 2^m * 4096 - 1.
All inputs are finite; a program needn't handle non-finite values.
Results may differ from the reference program's by a relative error of at most 0.00012.
Values sent between devices are 32-bit elements; how exact they have to be, the bound alone decides.
No kernel may reach another device: no remote copies, remote signals or barrier semaphores. Data moves between devices by JAX's collectives and lax.ppermute only.
A program may use at most 64 MiB of HBM per device.

```python
import jax
import jax.numpy as jnp
import numpy as np
from jax import lax

S = 4096
NRHS = 128
K = 2048
PANELS = 4
LEVELS = 3
SLOTS = 7
PAIRS = 3


def level_of_slot(slot_ids):
    level_ids = jnp.zeros_like(slot_ids)
    for power in range(1, (2 * PANELS).bit_length()):
        level_ids = level_ids + (slot_ids + 1 >= 2 ** power).astype(jnp.int32)
    return level_ids


def draw_diag_inverse(key, part):
    key_noise, key_diag = jax.random.split(key)
    slot_ids = jnp.arange(SLOTS, dtype=jnp.int32)
    level_ids = level_of_slot(slot_ids)
    span_sizes = jnp.left_shift(jnp.int32(1), level_ids)
    column_panel = slot_ids + 1 - span_sizes
    panel_ids = jnp.arange(PANELS, dtype=jnp.int32)
    row_panel = panel_ids[:, None] % span_sizes[None, :]
    dense_part = (column_panel[None, :] < row_panel)[:, None, :, None]
    on_block = (column_panel[None, :] == row_panel)[:, None, :, None]
    shape = (PANELS, S, SLOTS, S)
    noise = jax.random.normal(key_noise, shape, jnp.float32)
    diag_values = jnp.exp(jax.random.uniform(key_diag, (PANELS, S, SLOTS, 1), jnp.float32, -0.6931472, 0.6931472))
    row_ids = jnp.arange(S, dtype=jnp.int32)
    strict_lower = (row_ids[:, None] > row_ids[None, :])[None, :, None, :]
    on_diag = (row_ids[:, None] == row_ids[None, :])[None, :, None, :]
    far_scale = (0.8 / jnp.sqrt(span_sizes.astype(jnp.float32) * S))[None, None, :, None]
    near_values = jnp.where(strict_lower, noise * (0.7 / np.sqrt(S)), 0.0) + jnp.where(on_diag, diag_values, 0.0)
    far_values = noise * far_scale
    return jnp.where(on_block, near_values, jnp.where(dense_part, far_values, 0.0)).astype(jnp.float32)


def draw_row_lists(key, part):
    upper_levels = []
    for low_level in range(LEVELS):
        for high_level in range(low_level + 1, LEVELS):
            upper_levels.append(high_level)
    upper_table = jnp.asarray(np.array(upper_levels, dtype=np.int32))
    span_sizes = jnp.left_shift(jnp.int32(1), upper_table)[:, None, None]
    key_panel, key_parity = jax.random.split(key)
    panel_pick = jax.random.randint(key_panel, (PAIRS, PANELS, K), 0, 1 << 20, dtype=jnp.int32) % span_sizes
    parity = jax.random.randint(key_parity, (PAIRS, PANELS, K), 0, 2, dtype=jnp.int32)
    entry_ids = jnp.arange(K, dtype=jnp.int32)[None, None, :]
    panel_pick = jnp.where(entry_ids == 0, 0, jnp.where(entry_ids == K - 1, span_sizes - 1, panel_pick))
    parity = jnp.where(entry_ids == 0, 0, jnp.where(entry_ids == K - 1, 1, parity))
    return (panel_pick * S + 2 * entry_ids + parity).astype(jnp.int32)


def steps_of(stream_key, dims, shards, smallest, largest):
    factor_of, own = 1.0, jax.random.fold_in(stream_key, 6)
    for axis_at, shards_of in shards:
        draws = jnp.exp(jax.random.uniform(jax.random.fold_in(own, axis_at), (shards_of,), jnp.float32, smallest / len(shards), largest / len(shards)))
        factor_of = factor_of * jnp.repeat(draws, dims[axis_at] // shards_of).reshape([-1 if axis == axis_at else 1 for axis in range(len(dims))])
    return factor_of


def centred(own_key, dims, width, most, cuts=(), held_as=jnp.bfloat16):
    loudness = steps_of(own_key, dims, cuts, -0.22, 0.18) if cuts else 1.0
    result = jax.random.normal(own_key, dims, jnp.float32) * width * loudness
    return jnp.minimum(jnp.maximum(result, -most), most).astype(held_as)


def setup_inputs(seed: int = 0) -> dict:
    streams_of = jax.random.split(jax.random.key(seed), 5)
    return {
        "pressure_rhs": centred(streams_of[0], (LEVELS, PANELS, S, NRHS), 1.0, 6.0, ((1, 4), (2, 16)), jnp.float32),
        "diag_inverse": draw_diag_inverse(jax.random.fold_in(streams_of[4], 71), 0),
        "factor_blocks": centred(streams_of[2], (PAIRS, PANELS, K, S), S ** -0.5, 0.09375, ((1, 4), (2, 16), (3, 4)), jnp.float32),
        "row_lists": draw_row_lists(jax.random.fold_in(streams_of[4], 71), 0),
    }


exact_mode = lax.Precision.HIGHEST


def pair_slot(low_level, high_level):
    return low_level * (LEVELS - 1) - low_level * (low_level - 1) // 2 + high_level - low_level - 1


def target_rows(row_lists, low_level, high_level):
    span_size = 2 ** high_level
    base_rows = (jnp.arange(PANELS, dtype=jnp.int32) // span_size) * (span_size * S)
    return (base_rows[:, None] + row_lists[pair_slot(low_level, high_level)]).astype(jnp.int32)


def reference(pressure_rhs, diag_inverse, factor_blocks, row_lists):
    totals = [jnp.zeros((PANELS * S, NRHS), jnp.float32) for level_num in range(LEVELS)]
    solved = []
    for level_num in range(LEVELS):
        span_size = 2 ** level_num
        right_side = pressure_rhs[level_num] - totals[level_num].reshape(PANELS, S, NRHS)
        diag_blocks = diag_inverse[:, :, span_size - 1:2 * span_size - 1, :]
        grouped = right_side.reshape(PANELS // span_size, span_size, S, NRHS)
        spread_rhs = jnp.repeat(grouped, span_size, axis=0)
        solved_level = jnp.einsum("pias,pasn->pin", diag_blocks, spread_rhs, precision=exact_mode)
        solved.append(solved_level)
        for high_level in range(level_num + 1, LEVELS):
            slot_index = pair_slot(level_num, high_level)
            update_rows = jnp.einsum("pks,psn->pkn", factor_blocks[slot_index], solved_level, precision=exact_mode)
            where_to = target_rows(row_lists, level_num, high_level).reshape(-1)
            totals[high_level] = totals[high_level].at[where_to].add(update_rows.reshape(-1, NRHS))
    results = [None] * LEVELS
    for level_num in reversed(range(LEVELS)):
        span_size = 2 ** level_num
        residue = solved[level_num]
        for high_level in range(level_num + 1, LEVELS):
            slot_index = pair_slot(level_num, high_level)
            where_from = target_rows(row_lists, level_num, high_level)
            picked = results[high_level].reshape(PANELS * S, NRHS)[where_from]
            residue = residue - jnp.einsum("pks,pkn->psn", factor_blocks[slot_index], picked, precision=exact_mode)
        diag_blocks = diag_inverse[:, :, span_size - 1:2 * span_size - 1, :]
        pieces = jnp.einsum("pias,pin->pasn", diag_blocks, residue, precision=exact_mode)
        summed = pieces.reshape(PANELS // span_size, span_size, span_size, S, NRHS).sum(axis=1)
        results[level_num] = summed.reshape(PANELS, S, NRHS)
    return jnp.stack(results)
```

```python
import jax
import jax.numpy as jnp
from jax import lax
from jax.sharding import PartitionSpec as P

S = 4096
NRHS = 128
mode = lax.Precision.HIGH


def swapped(value, axis, mask):
    pairs = [(source, source ^ mask) for source in range(lax.axis_size(axis))]
    return lax.ppermute(value, axis, pairs)


def col_sum(part):
    cols = lax.axis_size("col")
    blocks = part.reshape(cols, -1, NRHS)
    own = lax.all_to_all(blocks, "col", 0, 0).sum(0)
    full = lax.all_to_all(jnp.broadcast_to(own, blocks.shape), "col", 0, 0)
    return full.reshape(part.shape)


def row_sum(part):
    part = part + swapped(part, "row", 1)
    return part + swapped(part, "row", 2)


def spread(update, lists, panels):
    keep = (lists // S == jnp.arange(panels)[:, None])[:, :, None] & (
        (lists % 2)[:, None] == jnp.arange(2)
    )
    placed = jnp.where(keep[..., None], update[None, :, None, :], 0.0)
    return placed.reshape(panels, -1, NRHS)


def pick(values, lists):
    panels = values.shape[0]
    keep = (lists // S == jnp.arange(panels)[:, None])[:, :, None] & (
        (lists % 2)[:, None] == jnp.arange(2)
    )
    parts = values.reshape(panels, -1, 2, NRHS)
    return jnp.where(keep[..., None], parts, 0.0).sum((0, 2))


def on_device(pressure_rhs, diag_inverse, factor_blocks, row_lists):
    sub = lax.axis_index("sub")
    rhs = pressure_rhs[:, 0]
    diag = diag_inverse[0]
    factor = factor_blocks[:, 0]
    lists = row_lists[:, 0]
    col_block = rhs.shape[1]

    packed = jnp.concatenate(
        [
            rhs[1:].reshape(-1, NRHS),
            lists.astype(jnp.float32),
            jnp.zeros((5, NRHS), jnp.float32),
        ]
    )
    seen = jnp.stack([packed] + [swapped(packed, "sub", m) for m in (1, 2, 3)])
    order = jnp.arange(4) ^ sub
    seen = seen[order]
    rhs_all = seen[:, : 2 * col_block].reshape(4, 2, col_block, NRHS)
    lists_all = seen[:, 2 * col_block : 2 * col_block + 3].astype(jnp.int32)
    mate = sub ^ 1

    def forward(level, right):
        first = 2**level - 1
        blocks = diag[:, first : first + 2**level, :]
        part = jnp.einsum("ias,asn->in", blocks, right, precision=mode)
        return col_sum(part)

    def backward(level, residue):
        first = 2**level - 1
        blocks = diag[:, first : first + 2**level, :]
        return jnp.einsum("ias,in->asn", blocks, residue, precision=mode)

    def update(slot, solved):
        return jnp.dot(factor[slot], solved, precision=mode)

    def correct(slot, picked):
        return jnp.einsum("ks,kn->sn", factor[slot], picked, precision=mode)

    y0 = forward(0, rhs[:1])
    u01 = row_sum(update(0, y0))
    u02 = update(1, y0)
    other = swapped(u01, "sub", 1)
    base = sub // 2 * 2
    rhs1 = lax.dynamic_slice_in_dim(rhs_all[:, 0], base, 2, 0)
    b1 = rhs1 - spread(u01, lists[0], 2) - spread(other, lists_all[mate, 0], 2)
    y1 = forward(1, b1)
    u2 = row_sum(jnp.concatenate([u02, update(2, y1)]))
    b2 = rhs_all[:, 1]
    for m in range(4):
        far = swapped(u2, "sub", m) if m else u2
        from_lists = lists_all[sub ^ m]
        b2 = b2 - spread(far[:NRHS], from_lists[1], 4) - spread(far[NRHS:], from_lists[2], 4)
    y2 = forward(2, b2)

    pieces2 = backward(2, y2)
    wanted = jnp.stack(
        [
            jnp.concatenate(
                [pick(pieces2, lists_all[s, 1]), pick(pieces2, lists_all[s, 2]), pieces2[s]]
            )
            for s in range(4)
        ]
    )
    mine = lax.all_to_all(wanted, "sub", 0, 0).sum(0)
    mine = row_sum(mine)
    pick02, pick12, x2 = mine[:NRHS], mine[NRHS : 2 * NRHS], mine[2 * NRHS :]
    w1 = y1 - col_sum(correct(2, pick12))
    pieces1 = backward(1, w1)
    keep = lax.dynamic_index_in_dim(pieces1, sub % 2, 0, keepdims=False)
    give = lax.dynamic_index_in_dim(pieces1, 1 - sub % 2, 0, keepdims=False)
    keep = jnp.concatenate([pick(pieces1, lists[0]), keep])
    give = jnp.concatenate([pick(pieces1, lists_all[mate, 0]), give])
    mine1 = row_sum(keep + swapped(give, "sub", 1))
    pick01, x1 = mine1[:NRHS], mine1[NRHS:]
    w0 = y0 - col_sum(correct(0, pick01) + correct(1, pick02))
    x0 = row_sum(backward(0, w0)[0])
    return jnp.stack([x0, x1, x2])[:, None]


def solution(mesh):
    in_specs = (
        P(None, "sub", "col", None),
        P("sub", "row", None, "col"),
        P(None, "sub", "col", "row"),
        P(None, "sub", "col"),
    )
    out_specs = P(None, "sub", "col", None)
    return jax.shard_map(
        on_device, mesh=mesh, in_specs=in_specs, out_specs=out_specs, check_vma=False
    )
```

```python
import functools

import jax
import jax.numpy as jnp
from jax import lax
from jax.experimental import pallas as pl
from jax.experimental.pallas import tpu as pltpu
from jax.sharding import PartitionSpec as P

S = 4096
N = 128
C = 256
R = 1024
K = 128
STEP = 256
LIST_AT = 2 * C
PACKED = 2 * C + 8
mode = lax.Precision.HIGH


def halves(value):
    high = value.astype(jnp.bfloat16)
    low = (value - high.astype(jnp.float32)).astype(jnp.bfloat16)
    return high, low


def mm(a, b):
    return jnp.dot(a, b, preferred_element_type=jnp.float32)


def hits(seen_ref, place, slots, panels):
    targets = jnp.concatenate(
        [seen_ref[place, LIST_AT + t : LIST_AT + t + 1, :] for t in slots], axis=1
    ).astype(jnp.int32)
    shape = (panels * C, K * len(slots))
    rows = lax.broadcasted_iota(jnp.int32, shape, 0)
    return jnp.where(rows == targets, 1.0, 0.0).astype(jnp.bfloat16)


SLOTS_OF = {1: (0,), 2: (1, 2)}


def forward_kernel(level, sub_ref, *refs):
    spans = 2**level
    updates = spans if level else 0
    seen_ref, refs = refs[0], refs[1:]
    update_refs, refs = refs[:updates], refs[updates:]
    diag_refs, (out_ref, right_ref) = refs[:spans], refs[spans:]

    @pl.when(pl.program_id(0) == 0)
    def _():
        if level == 0:
            high, low = halves(seen_ref[...])
            right_ref[0] = jnp.concatenate([high, low], axis=1)
        else:
            sub = sub_ref[0] % spans
            total = None
            for m in range(spans):
                high, low = halves(update_refs[m][...])
                pair = jnp.concatenate([high, low], axis=1)
                term = mm(hits(seen_ref, m, SLOTS_OF[level], spans), pair)
                total = term if total is None else total + term
            total = total[:, :N] + total[:, N:]
            for a in range(spans):
                rhs = seen_ref[a ^ sub, (level - 1) * C : level * C, :]
                high, low = halves(rhs - total[a * C : (a + 1) * C])
                right_ref[a] = jnp.concatenate([high, low], axis=1)

    wide, thin = None, None
    for a in range(spans):
        high, low = halves(diag_refs[a][0])
        one, two = mm(high, right_ref[a]), mm(low, right_ref[a, :, :N])
        wide = one if wide is None else wide + one
        thin = two if thin is None else thin + two
    out_ref[...] = wide[:, :N] + wide[:, N:] + thin


def diag_specs(level):
    spans = 2**level
    return [
        pl.BlockSpec((1, STEP, C), lambda i, s, a=a: (spans - 1 + a, i, 0)) for a in range(spans)
    ]


def whole(*shape):
    return pl.BlockSpec(shape, lambda i, s: (0,) * len(shape))


def forward(level, sub, seen, updates, diag):
    spans = 2**level
    return pl.pallas_call(
        functools.partial(forward_kernel, level),
        grid_spec=pltpu.PrefetchScalarGridSpec(
            num_scalar_prefetch=1,
            grid=(R // STEP,),
            in_specs=[whole(*seen.shape)] + [whole(*u.shape) for u in updates] + diag_specs(level),
            out_specs=pl.BlockSpec((STEP, N), lambda i, s: (i, 0)),
            scratch_shapes=[pltpu.VMEM((spans, C, 2 * N), jnp.bfloat16)],
        ),
        out_shape=jax.ShapeDtypeStruct((R, N), jnp.float32),
        cost_estimate=pl.CostEstimate(
            flops=6 * R * spans * C * N, bytes_accessed=4 * R * spans * C, transcendentals=0
        ),
        name=f"forward{level}",
    )(sub, seen, *updates, *[diag] * spans)


def backward_kernel(level, sub_ref, seen_ref, residue_ref, *refs):
    spans = 2**level
    diag_refs, refs = refs[:spans], refs[spans:]
    out_refs, total_ref = refs[:-1], refs[-1]
    step = pl.program_id(0)

    @pl.when(step == 0)
    def _():
        total_ref[...] = jnp.zeros_like(total_ref)

    high, low = halves(residue_ref[...].T)
    both = jnp.concatenate([high, low], axis=0)
    for a in range(spans):
        diag_high, diag_low = halves(diag_refs[a][0])
        one = mm(both, diag_high)
        total_ref[a] += one[:N] + one[N:] + mm(high, diag_low)

    @pl.when(step == R // STEP - 1)
    def _():
        if level == 0:
            out_refs[0][...] = total_ref[0].T
            return
        sub = sub_ref[0] % spans
        pieces = jnp.concatenate([total_ref[a] for a in range(spans)], axis=1)
        high, low = halves(pieces)
        both = jnp.concatenate([high, low], axis=0)
        for m in range(spans):
            picked = mm(both, hits(seen_ref, m, SLOTS_OF[level], spans))
            picked = (picked[:N] + picked[N:]).T
            own = total_ref[m ^ sub].T
            if level == 2:
                out_refs[2 * m][...] = picked[K:]
                out_refs[2 * m + 1][:K, :] = picked[:K]
                out_refs[2 * m + 1][K:, :] = own
            else:
                out_refs[m][:K, :] = picked
                out_refs[m][K:, :] = own


def backward(level, sub, seen, residue, diag):
    spans = 2**level
    heights = {0: [C], 1: [K + C] * 2, 2: [K, K + C] * 4}[level]
    return pl.pallas_call(
        functools.partial(backward_kernel, level),
        grid_spec=pltpu.PrefetchScalarGridSpec(
            num_scalar_prefetch=1,
            grid=(R // STEP,),
            in_specs=[whole(*seen.shape), pl.BlockSpec((STEP, N), lambda i, s: (i, 0))]
            + diag_specs(level),
            out_specs=[whole(h, N) for h in heights],
            scratch_shapes=[pltpu.VMEM((spans, N, C), jnp.float32)],
        ),
        out_shape=[jax.ShapeDtypeStruct((h, N), jnp.float32) for h in heights],
        cost_estimate=pl.CostEstimate(
            flops=6 * R * spans * C * N, bytes_accessed=4 * R * spans * C, transcendentals=0
        ),
        name=f"backward{level}",
    )(sub, seen, residue, *[diag] * spans)


def swapped(value, axis, mask):
    pairs = [(source, source ^ mask) for source in range(lax.axis_size(axis))]
    return lax.ppermute(value, axis, pairs)


def col_sum(part):
    cols = lax.axis_size("col")
    blocks = part.reshape(cols, -1, N)
    own = lax.all_to_all(blocks, "col", 0, 0).sum(0)
    full = lax.all_to_all(jnp.broadcast_to(own, blocks.shape), "col", 0, 0)
    return full.reshape(part.shape)


def row_sum(part):
    part = part + swapped(part, "row", 1)
    return part + swapped(part, "row", 2)


def on_device(pressure_rhs, diag_inverse, factor_blocks, row_lists):
    sub = lax.axis_index("sub").astype(jnp.int32).reshape(1)
    rhs = pressure_rhs[:, 0]
    diag = diag_inverse[0].transpose(1, 0, 2)
    factor = factor_blocks[:, 0]
    lists = row_lists[:, 0]
    targets = lists // S * C + lists % S - lax.axis_index("col") * C

    packed = jnp.concatenate(
        [
            rhs[1:].reshape(-1, N),
            targets.astype(jnp.float32),
            jnp.zeros((PACKED - LIST_AT - 3, N), jnp.float32),
        ]
    )
    seen = jnp.stack([packed] + [swapped(packed, "sub", m) for m in (1, 2, 3)])

    def update(slot, solved):
        return jnp.dot(factor[slot], solved, precision=mode)

    def correct(slot, picked):
        return jnp.einsum("ks,kn->sn", factor[slot], picked, precision=mode)

    y0 = col_sum(forward(0, sub, rhs[0], [], diag))
    u01 = row_sum(update(0, y0))
    u02 = update(1, y0)
    y1 = col_sum(forward(1, sub, seen, [u01, swapped(u01, "sub", 1)], diag))
    u2 = row_sum(jnp.concatenate([u02, update(2, y1)]))
    far = [swapped(u2, "sub", m) for m in (1, 2, 3)]
    y2 = col_sum(forward(2, sub, seen, [u2] + far, diag))

    out2 = backward(2, sub, seen, y2, diag)
    soon, later = list(out2[0::2]), list(out2[1::2])
    pick12 = row_sum(soon[0] + sum(swapped(soon[m], "sub", m) for m in (1, 2, 3)))
    pick12, *later = lax.optimization_barrier([pick12] + later)
    later = row_sum(later[0] + sum(swapped(later[m], "sub", m) for m in (1, 2, 3)))
    pick02, x2 = later[:K], later[K:]
    w1 = y1 - col_sum(correct(2, pick12))
    near, away = backward(1, sub, seen, w1, diag)
    mine = row_sum(near + swapped(away, "sub", 1))
    pick01, x1 = mine[:K], mine[K:]
    w0 = y0 - col_sum(correct(0, pick01) + correct(1, pick02))
    (x0,) = backward(0, sub, rhs[0], w0, diag)
    x0 = row_sum(x0)
    return jnp.stack([x0, x1, x2])[:, None]


def solution(mesh):
    in_specs = (
        P(None, "sub", "col", None),
        P("sub", "row", None, "col"),
        P(None, "sub", "col", "row"),
        P(None, "sub", "col"),
    )
    out_specs = P(None, "sub", "col", None)
    return jax.shard_map(
        on_device, mesh=mesh, in_specs=in_specs, out_specs=out_specs, check_vma=False
    )
```

```python
import functools

import jax
import jax.numpy as jnp
from jax import lax
from jax.experimental import pallas as pl
from jax.experimental.pallas import tpu as pltpu
from jax.sharding import PartitionSpec as P

S = 4096
N = 128
C = 256
R = 1024
K = 128
STEP = 256
LEVELS = 3
VMEM_LIMIT = 46 * 2**20
FIRST_LIMIT = 58 * 2**20
LIST_AT = 2 * C
PACKED = 2 * C + 8
mode = lax.Precision.HIGH


def halves(value):
    high = value.astype(jnp.bfloat16)
    low = (value - high.astype(jnp.float32)).astype(jnp.bfloat16)
    return high, low


def mm(a, b):
    return jnp.dot(a, b, preferred_element_type=jnp.float32)


def hits(seen_ref, place, slots, panels):
    targets = jnp.concatenate(
        [seen_ref[place, LIST_AT + t : LIST_AT + t + 1, :] for t in slots], axis=1
    ).astype(jnp.int32)
    shape = (panels * C, K * len(slots))
    rows = lax.broadcasted_iota(jnp.int32, shape, 0)
    return jnp.where(rows == targets, 1.0, 0.0).astype(jnp.bfloat16)


SLOTS_OF = {1: (0,), 2: (1, 2)}


def piece(spans, step, diag_ref, buffer_ref, sems):
    rows = pl.ds(pl.multiple_of(step * STEP, STEP), STEP)
    source = diag_ref.at[pl.ds(spans - 1, spans), rows, :]
    return pltpu.make_async_copy(source, buffer_ref.at[:, rows, :], sems.at[step])


def fetch(*refs):
    for step in range(R // STEP):
        piece(refs[0], step, *refs[1:]).start()


def forward_kernel(level, sub_ref, seen_ref, *refs):
    spans = 2**level
    update_refs, (diag_ref, out_ref, right_ref, buffer_ref, sems) = refs[:-5], refs[-5:]
    fetch(spans, diag_ref, buffer_ref, sems)
    if level == 0:
        high, low = halves(seen_ref[0])
        right_ref[0] = jnp.concatenate([high, low], axis=1)
    else:
        sub = sub_ref[0] % spans
        count = len(SLOTS_OF[level])
        total = None
        for m in range(spans):
            own = [update_refs[t * spans + m][...] for t in range(count)]
            high, low = halves(jnp.concatenate(own, axis=0))
            pair = jnp.concatenate([high, low], axis=1)
            term = mm(hits(seen_ref, m, SLOTS_OF[level], spans), pair)
            total = term if total is None else total + term
        total = total[:, :N] + total[:, N:]
        for a in range(spans):
            rhs = seen_ref[a ^ sub, (level - 1) * C : level * C, :]
            high, low = halves(rhs - total[a * C : (a + 1) * C])
            right_ref[a] = jnp.concatenate([high, low], axis=1)

    @pl.loop(0, R // STEP)
    def _(step):
        piece(spans, step, diag_ref, buffer_ref, sems).wait()
        rows = pl.ds(pl.multiple_of(step * STEP, STEP), STEP)
        wide, thin = None, None
        for a in range(spans):
            high, low = halves(buffer_ref[a, rows, :])
            one, two = mm(high, right_ref[a]), mm(low, right_ref[a, :, :N])
            wide = one if wide is None else wide + one
            thin = two if thin is None else thin + two
        out_ref[rows, :] = wide[:, :N] + wide[:, N:] + thin


def backward_kernel(level, sub_ref, seen_ref, base_ref, *refs):
    spans = 2**level
    minus = level < LEVELS - 1
    if minus:
        minus_ref, refs = refs[0], refs[1:]
    diag_ref, out_refs, (total_ref, buffer_ref, sems) = refs[0], refs[1:-3], refs[-3:]
    fetch(spans, diag_ref, buffer_ref, sems)
    total_ref[...] = jnp.zeros_like(total_ref)

    @pl.loop(0, R // STEP)
    def _(step):
        rows = pl.ds(pl.multiple_of(step * STEP, STEP), STEP)
        residue = base_ref[rows, :]
        if minus:
            residue = residue - minus_ref[rows, :]
        high, low = halves(residue.T)
        both = jnp.concatenate([high, low], axis=0)
        piece(spans, step, diag_ref, buffer_ref, sems).wait()
        for a in range(spans):
            diag_high, diag_low = halves(buffer_ref[a, rows, :])
            one = mm(both, diag_high)
            total_ref[a] += one[:N] + one[N:] + mm(high, diag_low)

    if level == 0:
        out_refs[0][...] = total_ref[0].T
        return
    sub = sub_ref[0] % spans
    pieces = jnp.concatenate([total_ref[a] for a in range(spans)], axis=1)
    high, low = halves(pieces)
    both = jnp.concatenate([high, low], axis=0)
    for m in range(spans):
        picked = mm(both, hits(seen_ref, m, SLOTS_OF[level], spans))
        picked = (picked[:N] + picked[N:]).T
        own = total_ref[m ^ sub].T
        soon_ref, later_ref = out_refs[2 * m], out_refs[2 * m + 1]
        if level == 2:
            soon_ref[...] = picked[K:]
            later_ref[:K, :] = picked[:K]
            later_ref[K:, :] = own
        else:
            soon_ref[...] = picked
            later_ref[...] = own


def call(kernel, level, heights, scratch, sub, *arrays):
    spans = 2**level
    vmem = pl.BlockSpec(memory_space=pltpu.VMEM)
    limit = FIRST_LIMIT if len(arrays) == 2 else VMEM_LIMIT
    specs = [vmem] * (len(arrays) - 1) + [pl.BlockSpec(memory_space=pltpu.HBM)]
    return pl.pallas_call(
        functools.partial(kernel, level),
        in_specs=[pl.BlockSpec(memory_space=pltpu.SMEM)] + specs,
        out_specs=[vmem] * len(heights),
        scratch_shapes=[
            scratch,
            pltpu.VMEM((spans, R, C), jnp.float32),
            pltpu.SemaphoreType.DMA((R // STEP,)),
        ],
        out_shape=[jax.ShapeDtypeStruct((h, N), jnp.float32) for h in heights],
        compiler_params=pltpu.CompilerParams(vmem_limit_bytes=limit),
        cost_estimate=pl.CostEstimate(
            flops=6 * R * spans * C * N, bytes_accessed=4 * R * spans * C, transcendentals=0
        ),
        name=f"{kernel.__name__}{level}",
    )(sub, *arrays)


def forward(level, sub, seen, updates, diag):
    scratch = pltpu.VMEM((2**level, C, 2 * N), jnp.bfloat16)
    return call(forward_kernel, level, [R], scratch, sub, seen, *updates, diag)[0]


def backward(level, sub, seen, residue, diag):
    heights = {0: [C], 1: [K, C] * 2, 2: [K, K + C] * 4}[level]
    scratch = pltpu.VMEM((2**level, N, C), jnp.float32)
    return call(backward_kernel, level, heights, scratch, sub, seen, *residue, diag)


def correct_kernel(slots, *refs):
    picked_refs, factor_ref, out_ref = refs[:-2], refs[-2], refs[-1]
    pairs = []
    for index in range(len(slots)):
        own, core, chip, both = (ref[...] for ref in picked_refs[4 * index : 4 * index + 4])
        pairs.append(halves((own + core) + (chip + both)))
    @pl.loop(0, R // STEP)
    def _(step):
        cols = pl.ds(pl.multiple_of(step * STEP, STEP), STEP)
        total = None
        for slot, (picked_high, picked_low) in zip(slots, pairs):
            high, low = halves(factor_ref[slot, :, cols].T)
            wide = mm(high, jnp.concatenate([picked_high, picked_low], axis=1))
            term = wide[:, :N] + wide[:, N:] + mm(low, picked_high)
            total = term if total is None else total + term
        out_ref[cols, :] = total


def correct(slots, picked, factor):
    vmem = pl.BlockSpec(memory_space=pltpu.VMEM)
    return pl.pallas_call(
        functools.partial(correct_kernel, slots),
        in_specs=[vmem] * (len(picked) + 1),
        out_specs=vmem,
        out_shape=jax.ShapeDtypeStruct((R, N), jnp.float32),
        compiler_params=pltpu.CompilerParams(vmem_limit_bytes=8 * 2**20),
        cost_estimate=pl.CostEstimate(
            flops=6 * R * K * N * len(slots), bytes_accessed=4 * R * K, transcendentals=0
        ),
        name=f"correct{len(slots)}",
    )(*picked, factor)


def swapped(value, axis, mask):
    pairs = [(source, source ^ mask) for source in range(lax.axis_size(axis))]
    return lax.ppermute(value, axis, pairs)


def col_sum(part, held=None):
    blocks = part.reshape(lax.axis_size("col"), -1, N)
    own = lax.all_to_all(blocks, "col", 0, 0).sum(0)
    if held is not None:
        own, held = lax.optimization_barrier((own, held))
    full = lax.all_to_all(jnp.broadcast_to(own, blocks.shape), "col", 0, 0)
    full = full.reshape(part.shape)
    return full if held is None else (full, held)


def row_parts(part):
    return [part] + [swapped(part, "row", m) for m in (1, 2, 3)]


def row_sum(part):
    own, core, chip, both = row_parts(part)
    return (own + core) + (chip + both)


def sub_parts(part):
    return [part] + [swapped(part, "sub", m) for m in (1, 2, 3)]


def sub_sum(parts):
    return parts[0] + sum(swapped(parts[m], "sub", m) for m in range(1, len(parts)))


def on_device(pressure_rhs, diag_inverse, factor_blocks, row_lists):
    sub = lax.axis_index("sub").astype(jnp.int32).reshape(1)
    rhs = pressure_rhs[:, 0]
    diag = diag_inverse[0].transpose(1, 0, 2)
    factor = factor_blocks[:, 0]
    lists = row_lists[:, 0]
    targets = lists // S * C + lists % S - lax.axis_index("col") * C

    packed = jnp.concatenate(
        [
            rhs[1:].reshape(-1, N),
            targets.astype(jnp.float32),
            jnp.zeros((PACKED - LIST_AT - 3, N), jnp.float32),
        ]
    )
    def update(slot, solved):
        return jnp.dot(factor[slot], solved, precision=mode)

    y0, packed = col_sum(forward(0, sub, rhs, [], diag), packed)
    seen = jnp.stack(sub_parts(packed))
    u01 = row_sum(update(0, y0))
    part1 = forward(1, sub, seen, [u01, swapped(u01, "sub", 1)], diag)
    part1, u02 = lax.optimization_barrier((part1, update(1, y0)))
    u02 = sub_parts(row_sum(u02))
    y1 = col_sum(part1)
    u12 = sub_parts(row_sum(update(2, y1)))
    y2 = col_sum(forward(2, sub, seen, u02 + u12, diag))

    out2 = backward(2, sub, seen, [y2], diag)
    pick12 = row_parts(sub_sum(out2[0::2]))
    part1, *later = lax.optimization_barrier([correct((2,), pick12, factor)] + list(out2[1::2]))
    later = row_sum(sub_sum(later))
    pick02, x2 = later[:K], later[K:]
    out1 = backward(1, sub, seen, [y1, col_sum(part1)], diag)
    pick01 = row_parts(sub_sum(out1[0::2]))
    zero = jnp.zeros_like(pick02)
    part0, *later = lax.optimization_barrier(
        [correct((0, 1), pick01 + [pick02, zero, zero, zero], factor)] + list(out1[1::2])
    )
    x1 = row_sum(sub_sum(later))
    (x0,) = backward(0, sub, rhs, [y0, col_sum(part0)], diag)
    x0 = row_sum(x0)
    return jnp.stack([x0, x1, x2])[:, None]


def solution(mesh):
    in_specs = (
        P(None, "sub", "col", None),
        P("sub", "row", None, "col"),
        P(None, "sub", "col", "row"),
        P(None, "sub", "col"),
    )
    out_specs = P(None, "sub", "col", None)
    return jax.shard_map(
        on_device, mesh=mesh, in_specs=in_specs, out_specs=out_specs, check_vma=False
    )
```

```python
import functools

import jax
import jax.numpy as jnp
from jax import lax
from jax.experimental import pallas as pl
from jax.experimental.pallas import tpu as pltpu
from jax.sharding import PartitionSpec as P

S = 4096
N = 128
C = 256
R = 1024
K = 128
STEP = 256
LEVELS = 3
VMEM_LIMIT = 46 * 2**20
FIRST_LIMIT = 48 * 2**20
LIST_AT = 2 * C
PACKED = 2 * C + 8
mode = lax.Precision.HIGH


def halves(value):
    high = value.astype(jnp.bfloat16)
    low = (value - high.astype(jnp.float32)).astype(jnp.bfloat16)
    return high, low


def mm(a, b):
    return jnp.dot(a, b, preferred_element_type=jnp.float32)


def hits(seen_ref, place, slots, panels):
    targets = jnp.concatenate(
        [seen_ref[place, LIST_AT + t : LIST_AT + t + 1, :] for t in slots], axis=1
    ).astype(jnp.int32)
    shape = (panels * C, K * len(slots))
    rows = lax.broadcasted_iota(jnp.int32, shape, 0)
    return jnp.where(rows == targets, 1.0, 0.0).astype(jnp.bfloat16)


SLOTS_OF = {1: (0,), 2: (1, 2)}


def piece(spans, step, diag_ref, buffer_ref, sems):
    rows = pl.ds(pl.multiple_of(step * STEP, STEP), STEP)
    source = diag_ref.at[pl.ds(spans - 1, spans), rows, :]
    return pltpu.make_async_copy(source, buffer_ref.at[:, rows, :], sems.at[step])


def fetch(*refs):
    for step in range(R // STEP):
        piece(refs[0], step, *refs[1:]).start()


def forward_kernel(level, sub_ref, seen_ref, *refs):
    spans = 2**level
    update_refs, (diag_ref, out_ref, right_ref, buffer_ref, sems) = refs[:-5], refs[-5:]
    fetch(spans, diag_ref, buffer_ref, sems)
    if level == 0:
        high, low = halves(seen_ref[0])
        right_ref[0] = jnp.concatenate([high, low], axis=1)
    else:
        sub = sub_ref[0] % spans
        total = None
        for m in range(spans):
            if level == 1:
                own = update_refs[m][...]
            else:
                early = update_refs[0][m * K : (m + 1) * K, :]
                own = jnp.concatenate([early, update_refs[m + 1][...]], axis=0)
            high, low = halves(own)
            pair = jnp.concatenate([high, low], axis=1)
            term = mm(hits(seen_ref, m, SLOTS_OF[level], spans), pair)
            total = term if total is None else total + term
        total = total[:, :N] + total[:, N:]
        for a in range(spans):
            rhs = seen_ref[a ^ sub, (level - 1) * C : level * C, :]
            high, low = halves(rhs - total[a * C : (a + 1) * C])
            right_ref[a] = jnp.concatenate([high, low], axis=1)

    @pl.loop(0, R // STEP)
    def _(step):
        piece(spans, step, diag_ref, buffer_ref, sems).wait()
        rows = pl.ds(pl.multiple_of(step * STEP, STEP), STEP)
        wide, thin = None, None
        for a in range(spans):
            high, low = halves(buffer_ref[a, rows, :])
            one, two = mm(high, right_ref[a]), mm(low, right_ref[a, :, :N])
            wide = one if wide is None else wide + one
            thin = two if thin is None else thin + two
        out_ref[rows, :] = wide[:, :N] + wide[:, N:] + thin


def backward_kernel(level, sub_ref, seen_ref, base_ref, *refs):
    spans = 2**level
    minus = level < LEVELS - 1
    if minus:
        minus_ref, refs = refs[0], refs[1:]
    diag_ref, out_refs, (total_ref, buffer_ref, sems) = refs[0], refs[1:-3], refs[-3:]
    fetch(spans, diag_ref, buffer_ref, sems)
    total_ref[...] = jnp.zeros_like(total_ref)

    @pl.loop(0, R // STEP)
    def _(step):
        rows = pl.ds(pl.multiple_of(step * STEP, STEP), STEP)
        residue = base_ref[rows, :]
        if minus:
            residue = residue - minus_ref[rows, :]
        high, low = halves(residue.T)
        both = jnp.concatenate([high, low], axis=0)
        piece(spans, step, diag_ref, buffer_ref, sems).wait()
        for a in range(spans):
            diag_high, diag_low = halves(buffer_ref[a, rows, :])
            one = mm(both, diag_high)
            total_ref[a] += one[:N] + one[N:] + mm(high, diag_low)

    if level == 0:
        out_refs[0][...] = total_ref[0].T
        return
    sub = sub_ref[0] % spans
    pieces = jnp.concatenate([total_ref[a] for a in range(spans)], axis=1)
    high, low = halves(pieces)
    both = jnp.concatenate([high, low], axis=0)
    for m in range(spans):
        picked = mm(both, hits(seen_ref, m, SLOTS_OF[level], spans))
        picked = (picked[:N] + picked[N:]).T
        own = total_ref[m ^ sub].T
        soon_ref, later_ref = out_refs[2 * m], out_refs[2 * m + 1]
        if level == 2:
            soon_ref[...] = picked[K:]
            later_ref[:K, :] = picked[:K]
            later_ref[K:, :] = own
        else:
            soon_ref[...] = picked
            later_ref[...] = own


def call(kernel, level, heights, scratch, sub, *arrays):
    spans = 2**level
    vmem = pl.BlockSpec(memory_space=pltpu.VMEM)
    limit = FIRST_LIMIT if len(arrays) == 2 else VMEM_LIMIT
    specs = [vmem] * (len(arrays) - 1) + [pl.BlockSpec(memory_space=pltpu.HBM)]
    return pl.pallas_call(
        functools.partial(kernel, level),
        in_specs=[pl.BlockSpec(memory_space=pltpu.SMEM)] + specs,
        out_specs=[vmem] * len(heights),
        scratch_shapes=[
            scratch,
            pltpu.VMEM((spans, R, C), jnp.float32),
            pltpu.SemaphoreType.DMA((R // STEP,)),
        ],
        out_shape=[jax.ShapeDtypeStruct((h, N), jnp.float32) for h in heights],
        compiler_params=pltpu.CompilerParams(vmem_limit_bytes=limit),
        cost_estimate=pl.CostEstimate(
            flops=6 * R * spans * C * N, bytes_accessed=4 * R * spans * C, transcendentals=0
        ),
        name=f"{kernel.__name__}{level}",
    )(sub, *arrays)


def forward(level, sub, seen, updates, diag):
    scratch = pltpu.VMEM((2**level, C, 2 * N), jnp.bfloat16)
    return call(forward_kernel, level, [R], scratch, sub, seen, *updates, diag)[0]


def backward(level, sub, seen, residue, diag):
    heights = {0: [C], 1: [K, C] * 2, 2: [K, K + C] * 4}[level]
    scratch = pltpu.VMEM((2**level, N, C), jnp.float32)
    return call(backward_kernel, level, heights, scratch, sub, seen, *residue, diag)


def correct_kernel(slots, *refs):
    picked_refs, factor_ref, out_ref = refs[:-2], refs[-2], refs[-1]
    pairs = []
    for index in range(len(slots)):
        own, core, chip, both = (ref[...] for ref in picked_refs[4 * index : 4 * index + 4])
        pairs.append(halves((own + core) + (chip + both)))
    @pl.loop(0, R // STEP)
    def _(step):
        cols = pl.ds(pl.multiple_of(step * STEP, STEP), STEP)
        total = None
        for slot, (picked_high, picked_low) in zip(slots, pairs):
            high, low = halves(factor_ref[slot, :, cols].T)
            wide = mm(high, jnp.concatenate([picked_high, picked_low], axis=1))
            term = wide[:, :N] + wide[:, N:] + mm(low, picked_high)
            total = term if total is None else total + term
        out_ref[cols, :] = total


def correct(slots, picked, factor):
    vmem = pl.BlockSpec(memory_space=pltpu.VMEM)
    return pl.pallas_call(
        functools.partial(correct_kernel, slots),
        in_specs=[vmem] * (len(picked) + 1),
        out_specs=vmem,
        out_shape=jax.ShapeDtypeStruct((R, N), jnp.float32),
        compiler_params=pltpu.CompilerParams(vmem_limit_bytes=8 * 2**20),
        cost_estimate=pl.CostEstimate(
            flops=6 * R * K * N * len(slots), bytes_accessed=4 * R * K, transcendentals=0
        ),
        name=f"correct{len(slots)}",
    )(*picked, factor)


def swapped(value, axis, mask):
    pairs = [(source, source ^ mask) for source in range(lax.axis_size(axis))]
    return lax.ppermute(value, axis, pairs)


def fold_kernel(parts_ref, out_ref):
    total = parts_ref[0]
    for place in range(1, parts_ref.shape[0]):
        total = total + parts_ref[place]
    for place in range(parts_ref.shape[0]):
        out_ref[place] = total


def fold(parts):
    vmem = pl.BlockSpec(memory_space=pltpu.VMEM)
    return pl.pallas_call(
        fold_kernel,
        in_specs=[vmem],
        out_specs=vmem,
        out_shape=jax.ShapeDtypeStruct(parts.shape, jnp.float32),
        compiler_params=pltpu.CompilerParams(vmem_limit_bytes=4 * 2**20),
        name="fold",
    )(parts)


def col_sum(part, *held):
    blocks = part.reshape(lax.axis_size("col"), -1, N)
    own, *held = lax.optimization_barrier((fold(lax.all_to_all(blocks, "col", 0, 0)), *held))
    full = lax.all_to_all(own, "col", 0, 0).reshape(part.shape)
    return (full, *held)


def row_parts(part):
    return [part] + [swapped(part, "row", m) for m in (1, 2, 3)]


def row_sum(part):
    own, core, chip, both = row_parts(part)
    return (own + core) + (chip + both)


def sub_parts(part):
    return [part] + [swapped(part, "sub", m) for m in (1, 2, 3)]


def sub_sum(parts):
    return parts[0] + sum(swapped(parts[m], "sub", m) for m in range(1, len(parts)))


def on_device(pressure_rhs, diag_inverse, factor_blocks, row_lists):
    sub = lax.axis_index("sub").astype(jnp.int32).reshape(1)
    rhs = pressure_rhs[:, 0]
    diag = diag_inverse[0].transpose(1, 0, 2)
    factor = factor_blocks[:, 0]
    lists = row_lists[:, 0]
    targets = lists // S * C + lists % S - lax.axis_index("col") * C

    packed = jnp.concatenate(
        [
            rhs[1:].reshape(-1, N),
            targets.astype(jnp.float32),
            jnp.zeros((PACKED - LIST_AT - 3, N), jnp.float32),
        ]
    )
    def update(slot, solved):
        return jnp.dot(factor[slot], solved, precision=mode)

    y0, packed = col_sum(forward(0, sub, rhs, [], diag), packed)
    seen = jnp.stack(sub_parts(packed))
    u01 = row_sum(update(0, y0))
    part1 = forward(1, sub, seen, [u01, swapped(u01, "sub", 1)], diag)
    part1, u02 = lax.optimization_barrier((part1, update(1, y0)))
    y1, u02 = col_sum(part1, row_sum(u02))
    y1, u02 = lax.optimization_barrier((y1, jnp.concatenate(sub_parts(u02))))
    u12 = sub_parts(row_sum(update(2, y1)))
    (y2,) = col_sum(forward(2, sub, seen, [u02] + u12, diag))

    out2 = backward(2, sub, seen, [y2], diag)
    pick12 = row_parts(sub_sum(out2[0::2]))
    part1, *later = lax.optimization_barrier([correct((2,), pick12, factor)] + list(out2[1::2]))
    later = row_sum(sub_sum(later))
    pick02, x2 = later[:K], later[K:]
    out1 = backward(1, sub, seen, [y1, *col_sum(part1)], diag)
    pick01 = row_parts(sub_sum(out1[0::2]))
    zero = jnp.zeros_like(pick02)
    part0, *later = lax.optimization_barrier(
        [correct((0, 1), pick01 + [pick02, zero, zero, zero], factor)] + list(out1[1::2])
    )
    x1 = row_sum(sub_sum(later))
    (x0,) = backward(0, sub, rhs, [y0, *col_sum(part0)], diag)
    x0 = row_sum(x0)
    return jnp.stack([x0, x1, x2])[:, None]


def solution(mesh):
    in_specs = (
        P(None, "sub", "col", None),
        P("sub", "row", None, "col"),
        P(None, "sub", "col", "row"),
        P(None, "sub", "col"),
    )
    out_specs = P(None, "sub", "col", None)
    return jax.shard_map(
        on_device, mesh=mesh, in_specs=in_specs, out_specs=out_specs, check_vma=False
    )
```

```python
import functools

import jax
import jax.numpy as jnp
from jax import lax
from jax.experimental import pallas as pl
from jax.experimental.pallas import tpu as pltpu
from jax.sharding import PartitionSpec as P

S = 4096
N = 128
C = 256
R = 1024
K = 128
STEP = 256
LEVELS = 3
VMEM_LIMIT = 46 * 2**20
FIRST_LIMIT = 48 * 2**20
LIST_AT = 2 * C
PACKED = 2 * C + 8
mode = lax.Precision.HIGH


def halves(value):
    high = value.astype(jnp.bfloat16)
    low = (value - high.astype(jnp.float32)).astype(jnp.bfloat16)
    return high, low


def mm(a, b):
    return jnp.dot(a, b, preferred_element_type=jnp.float32)


def hits(seen_ref, place, slots, panels):
    targets = jnp.concatenate(
        [seen_ref[place, LIST_AT + t : LIST_AT + t + 1, :] for t in slots], axis=1
    ).astype(jnp.int32)
    shape = (panels * C, K * len(slots))
    rows = lax.broadcasted_iota(jnp.int32, shape, 0)
    return jnp.where(rows == targets, 1.0, 0.0).astype(jnp.bfloat16)


SLOTS_OF = {1: (0,), 2: (1, 2)}


def piece(spans, step, diag_ref, buffer_ref, sems):
    rows = pl.ds(pl.multiple_of(step * STEP, STEP), STEP)
    source = diag_ref.at[pl.ds(spans - 1, spans), rows, :]
    return pltpu.make_async_copy(source, buffer_ref.at[:, rows, :], sems.at[step])


def fetch(*refs):
    for step in range(R // STEP):
        piece(refs[0], step, *refs[1:]).start()


def forward_kernel(level, sub_ref, seen_ref, *refs):
    spans = 2**level
    update_refs, (diag_ref, out_ref, right_ref, buffer_ref, sems) = refs[:-5], refs[-5:]
    fetch(spans, diag_ref, buffer_ref, sems)
    if level == 0:
        high, low = halves(seen_ref[0])
        right_ref[0] = jnp.concatenate([high, low], axis=1)
    else:
        sub = sub_ref[0] % spans
        total = None
        for m in range(spans):
            high, low = halves(update_refs[m][...])
            pair = jnp.concatenate([high, low], axis=1)
            term = mm(hits(seen_ref, m, SLOTS_OF[level], spans), pair)
            total = term if total is None else total + term
        total = total[:, :N] + total[:, N:]
        for a in range(spans):
            rhs = seen_ref[a ^ sub, (level - 1) * C : level * C, :]
            high, low = halves(rhs - total[a * C : (a + 1) * C])
            right_ref[a] = jnp.concatenate([high, low], axis=1)

    @pl.loop(0, R // STEP)
    def _(step):
        piece(spans, step, diag_ref, buffer_ref, sems).wait()
        rows = pl.ds(pl.multiple_of(step * STEP, STEP), STEP)
        wide, thin = None, None
        for a in range(spans):
            high, low = halves(buffer_ref[a, rows, :])
            one, two = mm(high, right_ref[a]), mm(low, right_ref[a, :, :N])
            wide = one if wide is None else wide + one
            thin = two if thin is None else thin + two
        out_ref[rows, :] = wide[:, :N] + wide[:, N:] + thin


def backward_kernel(level, sub_ref, seen_ref, base_ref, *refs):
    spans = 2**level
    minus = level < LEVELS - 1
    if minus:
        minus_ref, refs = refs[0], refs[1:]
    diag_ref, out_refs, (total_ref, buffer_ref, sems) = refs[0], refs[1:-3], refs[-3:]
    fetch(spans, diag_ref, buffer_ref, sems)
    total_ref[...] = jnp.zeros_like(total_ref)

    @pl.loop(0, R // STEP)
    def _(step):
        rows = pl.ds(pl.multiple_of(step * STEP, STEP), STEP)
        residue = base_ref[rows, :]
        if minus:
            residue = residue - minus_ref[rows, :]
        high, low = halves(residue.T)
        both = jnp.concatenate([high, low], axis=0)
        piece(spans, step, diag_ref, buffer_ref, sems).wait()
        for a in range(spans):
            diag_high, diag_low = halves(buffer_ref[a, rows, :])
            one = mm(both, diag_high)
            total_ref[a] += one[:N] + one[N:] + mm(high, diag_low)

    if level == 0:
        out_refs[0][...] = total_ref[0].T
        return
    sub = sub_ref[0] % spans
    pieces = jnp.concatenate([total_ref[a] for a in range(spans)], axis=1)
    high, low = halves(pieces)
    both = jnp.concatenate([high, low], axis=0)
    for m in range(spans):
        picked = mm(both, hits(seen_ref, m, SLOTS_OF[level], spans))
        picked = (picked[:N] + picked[N:]).T
        own = total_ref[m ^ sub].T
        soon_ref, later_ref = out_refs[2 * m], out_refs[2 * m + 1]
        if level == 2:
            soon_ref[...] = picked[K:]
            early_ref = out_refs[2 * spans + m]
            early_ref[...] = picked[:K]
            later_ref[...] = own
        else:
            soon_ref[...] = picked
            later_ref[...] = own


def call(kernel, level, heights, scratch, sub, *arrays):
    spans = 2**level
    vmem = pl.BlockSpec(memory_space=pltpu.VMEM)
    limit = FIRST_LIMIT if len(arrays) == 2 else VMEM_LIMIT
    specs = [vmem] * (len(arrays) - 1) + [pl.BlockSpec(memory_space=pltpu.HBM)]
    return pl.pallas_call(
        functools.partial(kernel, level),
        in_specs=[pl.BlockSpec(memory_space=pltpu.SMEM)] + specs,
        out_specs=[vmem] * len(heights),
        scratch_shapes=[
            scratch,
            pltpu.VMEM((spans, R, C), jnp.float32),
            pltpu.SemaphoreType.DMA((R // STEP,)),
        ],
        out_shape=[jax.ShapeDtypeStruct((h, N), jnp.float32) for h in heights],
        compiler_params=pltpu.CompilerParams(vmem_limit_bytes=limit),
        cost_estimate=pl.CostEstimate(
            flops=6 * R * spans * C * N, bytes_accessed=4 * R * spans * C, transcendentals=0
        ),
        name=f"{kernel.__name__}{level}",
    )(sub, *arrays)


def forward(level, sub, seen, updates, diag):
    scratch = pltpu.VMEM((2**level, C, 2 * N), jnp.bfloat16)
    return call(forward_kernel, level, [R], scratch, sub, seen, *updates, diag)[0]


def backward(level, sub, seen, residue, diag):
    heights = {0: [C], 1: [K, C] * 2, 2: [K, C] * 4 + [K] * 4}[level]
    scratch = pltpu.VMEM((2**level, N, C), jnp.float32)
    return call(backward_kernel, level, heights, scratch, sub, seen, *residue, diag)


def join_kernel(early_ref, solved_ref, factor_ref, out_ref):
    out_ref[:K, :] = early_ref[...]
    solved_high, solved_low = halves(solved_ref[...])
    high, low = halves(factor_ref[2])
    wide = mm(high, jnp.concatenate([solved_high, solved_low], axis=1))
    out_ref[K:, :] = wide[:, :N] + wide[:, N:] + mm(low, solved_high)


def join(early, solved, factor):
    vmem = pl.BlockSpec(memory_space=pltpu.VMEM)
    return pl.pallas_call(
        join_kernel,
        in_specs=[vmem] * 3,
        out_specs=vmem,
        out_shape=jax.ShapeDtypeStruct((2 * K, N), jnp.float32),
        compiler_params=pltpu.CompilerParams(vmem_limit_bytes=8 * 2**20),
        name="join",
    )(early, solved, factor)


def correct_kernel(slots, *refs):
    picked_refs, factor_ref, out_ref = refs[:-2], refs[-2], refs[-1]
    pairs = []
    for index in range(len(slots)):
        own, core, chip, both = (ref[...] for ref in picked_refs[4 * index : 4 * index + 4])
        pairs.append(halves((own + core) + (chip + both)))
    @pl.loop(0, R // STEP)
    def _(step):
        cols = pl.ds(pl.multiple_of(step * STEP, STEP), STEP)
        total = None
        for slot, (picked_high, picked_low) in zip(slots, pairs):
            high, low = halves(factor_ref[slot, :, cols].T)
            wide = mm(high, jnp.concatenate([picked_high, picked_low], axis=1))
            term = wide[:, :N] + wide[:, N:] + mm(low, picked_high)
            total = term if total is None else total + term
        out_ref[cols, :] = total


def correct(slots, picked, factor):
    vmem = pl.BlockSpec(memory_space=pltpu.VMEM)
    return pl.pallas_call(
        functools.partial(correct_kernel, slots),
        in_specs=[vmem] * (len(picked) + 1),
        out_specs=vmem,
        out_shape=jax.ShapeDtypeStruct((R, N), jnp.float32),
        compiler_params=pltpu.CompilerParams(vmem_limit_bytes=8 * 2**20),
        cost_estimate=pl.CostEstimate(
            flops=6 * R * K * N * len(slots), bytes_accessed=4 * R * K, transcendentals=0
        ),
        name=f"correct{len(slots)}",
    )(*picked, factor)


def swapped(value, axis, mask):
    pairs = [(source, source ^ mask) for source in range(lax.axis_size(axis))]
    return lax.ppermute(value, axis, pairs)


def fold_kernel(parts_ref, out_ref):
    total = parts_ref[0]
    for place in range(1, parts_ref.shape[0]):
        total = total + parts_ref[place]
    for place in range(parts_ref.shape[0]):
        out_ref[place] = total


def fold(parts):
    vmem = pl.BlockSpec(memory_space=pltpu.VMEM)
    return pl.pallas_call(
        fold_kernel,
        in_specs=[vmem],
        out_specs=vmem,
        out_shape=jax.ShapeDtypeStruct(parts.shape, jnp.float32),
        compiler_params=pltpu.CompilerParams(vmem_limit_bytes=4 * 2**20),
        name="fold",
    )(parts)


def col_sum(part, *held):
    blocks = part.reshape(lax.axis_size("col"), -1, N)
    own, *held = lax.optimization_barrier((fold(lax.all_to_all(blocks, "col", 0, 0)), *held))
    full = lax.all_to_all(own, "col", 0, 0).reshape(part.shape)
    return (full, *held)


def row_parts(part):
    return [part] + [swapped(part, "row", m) for m in (1, 2, 3)]


def row_sum(part):
    own, core, chip, both = row_parts(part)
    return (own + core) + (chip + both)


def sub_parts(part):
    return [part] + [swapped(part, "sub", m) for m in (1, 2, 3)]


def sub_sum(parts):
    return parts[0] + sum(swapped(parts[m], "sub", m) for m in range(1, len(parts)))


def on_device(pressure_rhs, diag_inverse, factor_blocks, row_lists):
    sub = lax.axis_index("sub").astype(jnp.int32).reshape(1)
    rhs = pressure_rhs[:, 0]
    diag = diag_inverse[0].transpose(1, 0, 2)
    factor = factor_blocks[:, 0]
    lists = row_lists[:, 0]
    targets = lists // S * C + lists % S - lax.axis_index("col") * C

    packed = jnp.concatenate(
        [
            rhs[1:].reshape(-1, N),
            targets.astype(jnp.float32),
            jnp.zeros((PACKED - LIST_AT - 3, N), jnp.float32),
        ]
    )

    def update(slot, solved):
        return jnp.dot(factor[slot], solved, precision=mode)

    y0, packed = col_sum(forward(0, sub, rhs, [], diag), packed)
    seen = jnp.stack(sub_parts(packed))
    u01 = row_sum(update(0, y0))
    part1 = forward(1, sub, seen, [u01, swapped(u01, "sub", 1)], diag)
    part1, u02 = lax.optimization_barrier((part1, update(1, y0)))
    (y1,) = col_sum(part1)
    u2 = sub_parts(row_sum(join(u02, y1, factor)))
    (y2,) = col_sum(forward(2, sub, seen, u2, diag))

    out2 = backward(2, sub, seen, [y2], diag)
    soon, later, early = out2[0:8:2], out2[1:8:2], out2[8:]
    pick12 = row_parts(sub_sum(soon))
    (part1, *early) = col_sum(correct((2,), pick12, factor), *early)
    part1, pick02 = lax.optimization_barrier((part1, row_sum(sub_sum(early))))
    out1 = backward(1, sub, seen, [y1, part1], diag)
    pick01 = row_parts(sub_sum(out1[0::2]))
    zero = jnp.zeros_like(pick02)
    part0 = correct((0, 1), pick01 + [pick02, zero, zero, zero], factor)
    (part0, *later) = col_sum(part0, *later, *out1[1::2])
    x12 = row_sum(jnp.concatenate([sub_sum(later[4:]), sub_sum(later[:4])]))
    (x0,) = backward(0, sub, rhs, [y0, part0], diag)
    x0 = row_sum(x0)
    return jnp.concatenate([x0, x12]).reshape(LEVELS, 1, C, N)


def solution(mesh):
    in_specs = (
        P(None, "sub", "col", None),
        P("sub", "row", None, "col"),
        P(None, "sub", "col", "row"),
        P(None, "sub", "col"),
    )
    out_specs = P(None, "sub", "col", None)
    return jax.shard_map(
        on_device, mesh=mesh, in_specs=in_specs, out_specs=out_specs, check_vma=False
    )
```

```python
import functools

import jax
import jax.numpy as jnp
from jax import lax
from jax.experimental import pallas as pl
from jax.experimental.pallas import tpu as pltpu
from jax.sharding import PartitionSpec as P

S = 4096
N = 128
C = 256
R = 1024
K = 128
STEP = 256
LEVELS = 3
VMEM_LIMIT = 46 * 2**20
FIRST_LIMIT = 48 * 2**20
LIST_AT = 2 * C
PACKED = 2 * C + 8
mode = lax.Precision.HIGH


def halves(value):
    high = value.astype(jnp.bfloat16)
    low = (value - high.astype(jnp.float32)).astype(jnp.bfloat16)
    return high, low


def mm(a, b):
    return jnp.dot(a, b, preferred_element_type=jnp.float32)


def hits(seen_ref, place, slots, panels):
    targets = jnp.concatenate(
        [seen_ref[place, LIST_AT + t : LIST_AT + t + 1, :] for t in slots], axis=1
    ).astype(jnp.int32)
    shape = (panels * C, K * len(slots))
    rows = lax.broadcasted_iota(jnp.int32, shape, 0)
    return jnp.where(rows == targets, 1.0, 0.0).astype(jnp.bfloat16)


SLOTS_OF = {1: (0,), 2: (1, 2)}


def piece(spans, step, diag_ref, buffer_ref, sems):
    rows = pl.ds(pl.multiple_of(step * STEP, STEP), STEP)
    source = diag_ref.at[pl.ds(spans - 1, spans), rows, :]
    return pltpu.make_async_copy(source, buffer_ref.at[:, rows, :], sems.at[step])


def fetch(*refs):
    for step in range(R // STEP):
        piece(refs[0], step, *refs[1:]).start()


def forward_kernel(level, sub_ref, seen_ref, *refs):
    spans = 2**level
    update_refs, (diag_ref, out_ref, right_ref, buffer_ref, sems) = refs[:-5], refs[-5:]
    fetch(spans, diag_ref, buffer_ref, sems)
    if level == 0:
        high, low = halves(seen_ref[0])
        right_ref[0] = jnp.concatenate([high, low], axis=1)
    else:
        sub = sub_ref[0] % spans
        total = None
        for m in range(spans):
            if level == 1:
                own = update_refs[m][...]
            else:
                early = update_refs[0][m * K : (m + 1) * K, :]
                own = jnp.concatenate([early, update_refs[m + 1][...]], axis=0)
            high, low = halves(own)
            pair = jnp.concatenate([high, low], axis=1)
            term = mm(hits(seen_ref, m, SLOTS_OF[level], spans), pair)
            total = term if total is None else total + term
        total = total[:, :N] + total[:, N:]
        for a in range(spans):
            rhs = seen_ref[a ^ sub, (level - 1) * C : level * C, :]
            high, low = halves(rhs - total[a * C : (a + 1) * C])
            right_ref[a] = jnp.concatenate([high, low], axis=1)

    @pl.loop(0, R // STEP)
    def _(step):
        piece(spans, step, diag_ref, buffer_ref, sems).wait()
        rows = pl.ds(pl.multiple_of(step * STEP, STEP), STEP)
        wide, thin = None, None
        for a in range(spans):
            high, low = halves(buffer_ref[a, rows, :])
            one, two = mm(high, right_ref[a]), mm(low, right_ref[a, :, :N])
            wide = one if wide is None else wide + one
            thin = two if thin is None else thin + two
        out_ref[rows, :] = wide[:, :N] + wide[:, N:] + thin


def backward_kernel(level, sub_ref, seen_ref, base_ref, *refs):
    spans = 2**level
    minus = level < LEVELS - 1
    if minus:
        minus_ref, refs = refs[0], refs[1:]
    diag_ref, out_refs, (total_ref, buffer_ref, sems) = refs[0], refs[1:-3], refs[-3:]
    fetch(spans, diag_ref, buffer_ref, sems)
    total_ref[...] = jnp.zeros_like(total_ref)

    @pl.loop(0, R // STEP)
    def _(step):
        rows = pl.ds(pl.multiple_of(step * STEP, STEP), STEP)
        residue = base_ref[rows, :]
        if minus:
            residue = residue - minus_ref[rows, :]
        high, low = halves(residue.T)
        both = jnp.concatenate([high, low], axis=0)
        piece(spans, step, diag_ref, buffer_ref, sems).wait()
        for a in range(spans):
            diag_high, diag_low = halves(buffer_ref[a, rows, :])
            one = mm(both, diag_high)
            total_ref[a] += one[:N] + one[N:] + mm(high, diag_low)

    if level == 0:
        out_refs[0][...] = total_ref[0].T
        return
    sub = sub_ref[0] % spans
    pieces = jnp.concatenate([total_ref[a] for a in range(spans)], axis=1)
    high, low = halves(pieces)
    both = jnp.concatenate([high, low], axis=0)
    for m in range(spans):
        picked = mm(both, hits(seen_ref, m, SLOTS_OF[level], spans))
        picked = (picked[:N] + picked[N:]).T
        own = total_ref[m ^ sub].T
        soon_ref, later_ref = out_refs[2 * m], out_refs[2 * m + 1]
        if level == 2:
            soon_ref[...] = picked[K:]
            later_ref[:K, :] = picked[:K]
            later_ref[K:, :] = own
        else:
            soon_ref[...] = picked
            later_ref[...] = own


def call(kernel, level, heights, scratch, sub, *arrays):
    spans = 2**level
    vmem = pl.BlockSpec(memory_space=pltpu.VMEM)
    limit = FIRST_LIMIT if len(arrays) == 2 else VMEM_LIMIT
    specs = [vmem] * (len(arrays) - 1) + [pl.BlockSpec(memory_space=pltpu.HBM)]
    return pl.pallas_call(
        functools.partial(kernel, level),
        in_specs=[pl.BlockSpec(memory_space=pltpu.SMEM)] + specs,
        out_specs=[vmem] * len(heights),
        scratch_shapes=[
            scratch,
            pltpu.VMEM((spans, R, C), jnp.float32),
            pltpu.SemaphoreType.DMA((R // STEP,)),
        ],
        out_shape=[jax.ShapeDtypeStruct((h, N), jnp.float32) for h in heights],
        compiler_params=pltpu.CompilerParams(vmem_limit_bytes=limit),
        cost_estimate=pl.CostEstimate(
            flops=6 * R * spans * C * N, bytes_accessed=4 * R * spans * C, transcendentals=0
        ),
        name=f"{kernel.__name__}{level}",
    )(sub, *arrays)


def forward(level, sub, seen, updates, diag):
    scratch = pltpu.VMEM((2**level, C, 2 * N), jnp.bfloat16)
    return call(forward_kernel, level, [R], scratch, sub, seen, *updates, diag)[0]


def backward(level, sub, seen, residue, diag):
    heights = {0: [C], 1: [K, C] * 2, 2: [K, K + C] * 4}[level]
    scratch = pltpu.VMEM((2**level, N, C), jnp.float32)
    return call(backward_kernel, level, heights, scratch, sub, seen, *residue, diag)


def correct_kernel(slots, *refs):
    picked_refs, factor_ref, out_ref = refs[:-2], refs[-2], refs[-1]
    own, core, chip, both = (ref[...] for ref in picked_refs)
    total = (own + core) + (chip + both)
    pairs = [halves(total[i * K : (i + 1) * K]) for i in range(len(slots))]

    @pl.loop(0, R // STEP)
    def _(step):
        cols = pl.ds(pl.multiple_of(step * STEP, STEP), STEP)
        total = None
        for slot, (picked_high, picked_low) in zip(slots, pairs):
            high, low = halves(factor_ref[slot, :, cols].T)
            wide = mm(high, jnp.concatenate([picked_high, picked_low], axis=1))
            term = wide[:, :N] + wide[:, N:] + mm(low, picked_high)
            total = term if total is None else total + term
        out_ref[cols, :] = total


def correct(slots, picked, factor):
    vmem = pl.BlockSpec(memory_space=pltpu.VMEM)
    return pl.pallas_call(
        functools.partial(correct_kernel, slots),
        in_specs=[vmem] * (len(picked) + 1),
        out_specs=vmem,
        out_shape=jax.ShapeDtypeStruct((R, N), jnp.float32),
        compiler_params=pltpu.CompilerParams(vmem_limit_bytes=8 * 2**20),
        cost_estimate=pl.CostEstimate(
            flops=6 * R * K * N * len(slots), bytes_accessed=4 * R * K, transcendentals=0
        ),
        name=f"correct{len(slots)}",
    )(*picked, factor)


def swapped(value, axis, mask):
    pairs = [(source, source ^ mask) for source in range(lax.axis_size(axis))]
    return lax.ppermute(value, axis, pairs)


def fold_kernel(parts_ref, out_ref):
    total = parts_ref[0]
    for place in range(1, parts_ref.shape[0]):
        total = total + parts_ref[place]
    for place in range(parts_ref.shape[0]):
        out_ref[place] = total


def fold(parts):
    vmem = pl.BlockSpec(memory_space=pltpu.VMEM)
    return pl.pallas_call(
        fold_kernel,
        in_specs=[vmem],
        out_specs=vmem,
        out_shape=jax.ShapeDtypeStruct(parts.shape, jnp.float32),
        compiler_params=pltpu.CompilerParams(vmem_limit_bytes=4 * 2**20),
        name="fold",
    )(parts)


def col_sum(part, *held):
    blocks = part.reshape(lax.axis_size("col"), -1, N)
    own, *held = lax.optimization_barrier((fold(lax.all_to_all(blocks, "col", 0, 0)), *held))
    full = lax.all_to_all(own, "col", 0, 0).reshape(part.shape)
    return (full, *held)


def row_parts(part):
    return [part] + [swapped(part, "row", m) for m in (1, 2, 3)]


def row_sum(part):
    own, core, chip, both = row_parts(part)
    return (own + core) + (chip + both)


def sub_parts(part):
    return [part] + [swapped(part, "sub", m) for m in (1, 2, 3)]


def sub_sum(parts):
    return parts[0] + sum(swapped(parts[m], "sub", m) for m in range(1, len(parts)))


def on_device(pressure_rhs, diag_inverse, factor_blocks, row_lists):
    sub = lax.axis_index("sub").astype(jnp.int32).reshape(1)
    rhs = pressure_rhs[:, 0]
    diag = diag_inverse[0].transpose(1, 0, 2)
    factor = factor_blocks[:, 0]
    lists = row_lists[:, 0]
    targets = lists // S * C + lists % S - lax.axis_index("col") * C

    packed = jnp.concatenate(
        [
            rhs[1:].reshape(-1, N),
            targets.astype(jnp.float32),
            jnp.zeros((PACKED - LIST_AT - 3, N), jnp.float32),
        ]
    )
    def update(slot, solved):
        return jnp.dot(factor[slot], solved, precision=mode)

    y0, packed = col_sum(forward(0, sub, rhs, [], diag), packed)
    seen = jnp.stack(sub_parts(packed))
    u01 = row_sum(update(0, y0))
    part1 = forward(1, sub, seen, [u01, swapped(u01, "sub", 1)], diag)
    part1, u02 = lax.optimization_barrier((part1, update(1, y0)))
    y1, u02 = col_sum(part1, row_sum(u02))
    y1, u02 = lax.optimization_barrier((y1, jnp.concatenate(sub_parts(u02))))
    u12 = sub_parts(row_sum(update(2, y1)))
    (y2,) = col_sum(forward(2, sub, seen, [u02] + u12, diag))

    out2 = backward(2, sub, seen, [y2], diag)
    pick12 = row_parts(sub_sum(out2[0::2]))
    part1, *later = lax.optimization_barrier([correct((2,), pick12, factor)] + list(out2[1::2]))
    later = sub_sum(later)
    out1 = backward(1, sub, seen, [y1, *col_sum(part1)], diag)
    picked = row_parts(jnp.concatenate([sub_sum(out1[0::2]), later[:K]]))
    part0, x2 = lax.optimization_barrier((correct((0, 1), picked, factor), later[K:]))
    part0, x2, *later = col_sum(part0, x2, *out1[1::2])
    x2 = row_sum(x2)
    x1 = row_sum(sub_sum(later))
    (x0,) = backward(0, sub, rhs, [y0, part0], diag)
    x0 = row_sum(x0)
    return jnp.stack([x0, x1, x2])[:, None]


def solution(mesh):
    in_specs = (
        P(None, "sub", "col", None),
        P("sub", "row", None, "col"),
        P(None, "sub", "col", "row"),
        P(None, "sub", "col"),
    )
    out_specs = P(None, "sub", "col", None)
    return jax.shard_map(
        on_device, mesh=mesh, in_specs=in_specs, out_specs=out_specs, check_vma=False
    )
```

```python
import functools

import jax
import jax.numpy as jnp
from jax import lax
from jax.experimental import pallas as pl
from jax.experimental.pallas import tpu as pltpu
from jax.sharding import PartitionSpec as P

S = 4096
N = 128
C = 256
R = 1024
K = 128
STEP = 256
LEVELS = 3
VMEM_LIMIT = 46 * 2**20
FIRST_LIMIT = 58 * 2**20
LIST_AT = 2 * C
PACKED = 2 * C + 8
mode = lax.Precision.HIGH


def halves(value):
    high = value.astype(jnp.bfloat16)
    low = (value - high.astype(jnp.float32)).astype(jnp.bfloat16)
    return high, low


def mm(a, b):
    return jnp.dot(a, b, preferred_element_type=jnp.float32)


def hits(seen_ref, place, slots, panels):
    targets = jnp.concatenate(
        [seen_ref[place, LIST_AT + t : LIST_AT + t + 1, :] for t in slots], axis=1
    ).astype(jnp.int32)
    shape = (panels * C, K * len(slots))
    rows = lax.broadcasted_iota(jnp.int32, shape, 0)
    return jnp.where(rows == targets, 1.0, 0.0).astype(jnp.bfloat16)


SLOTS_OF = {1: (0,), 2: (1, 2)}


def piece(spans, step, diag_ref, buffer_ref, sems):
    rows = pl.ds(pl.multiple_of(step * STEP, STEP), STEP)
    source = diag_ref.at[pl.ds(spans - 1, spans), rows, :]
    return pltpu.make_async_copy(source, buffer_ref.at[:, rows, :], sems.at[step])


def fetch(*refs):
    for step in range(R // STEP):
        piece(refs[0], step, *refs[1:]).start()


def forward_kernel(level, sub_ref, seen_ref, *refs):
    spans = 2**level
    if level:
        update_refs, (diag_ref, out_ref, right_ref, buffer_ref, sems) = refs[:-5], refs[-5:]
    else:
        diag_ref, out_ref, right_ref, buffer_ref, sems, plain_ref = refs
        first = pltpu.make_async_copy(seen_ref.at[0], plain_ref, sems.at[R // STEP])
        first.start()
    fetch(spans, diag_ref, buffer_ref, sems)
    if level == 0:
        first.wait()
        high, low = halves(plain_ref[...])
        right_ref[0] = jnp.concatenate([high, low], axis=1)
    else:
        sub = sub_ref[0] % spans
        total = None
        for m in range(spans):
            if level == 1:
                own = update_refs[m][...]
            else:
                early = update_refs[0][m * K : (m + 1) * K, :]
                own = jnp.concatenate([early, update_refs[m + 1][...]], axis=0)
            high, low = halves(own)
            pair = jnp.concatenate([high, low], axis=1)
            term = mm(hits(seen_ref, m, SLOTS_OF[level], spans), pair)
            total = term if total is None else total + term
        total = total[:, :N] + total[:, N:]
        for a in range(spans):
            rhs = seen_ref[a ^ sub, (level - 1) * C : level * C, :]
            high, low = halves(rhs - total[a * C : (a + 1) * C])
            right_ref[a] = jnp.concatenate([high, low], axis=1)

    @pl.loop(0, R // STEP)
    def _(step):
        piece(spans, step, diag_ref, buffer_ref, sems).wait()
        rows = pl.ds(pl.multiple_of(step * STEP, STEP), STEP)
        wide, thin = None, None
        for a in range(spans):
            high, low = halves(buffer_ref[a, rows, :])
            one, two = mm(high, right_ref[a]), mm(low, right_ref[a, :, :N])
            wide = one if wide is None else wide + one
            thin = two if thin is None else thin + two
        out_ref[rows, :] = wide[:, :N] + wide[:, N:] + thin


def backward_kernel(level, sub_ref, seen_ref, base_ref, *refs):
    spans = 2**level
    minus = level < LEVELS - 1
    count = 2 if minus else 1
    plain, refs = refs[-count:], refs[:-count]
    total_ref, buffer_ref, sems = refs[-3:]
    diag_ref, out_refs = refs[count - 1], refs[count:-3]
    pairs = list(zip([base_ref, refs[0]], plain))
    copies = [
        pltpu.make_async_copy(source, target, sems.at[R // STEP + i])
        for i, (source, target) in enumerate(pairs)
    ]
    for copy in copies:
        copy.start()
    fetch(spans, diag_ref, buffer_ref, sems)
    total_ref[...] = jnp.zeros_like(total_ref)
    for copy in copies:
        copy.wait()

    @pl.loop(0, R // STEP)
    def _(step):
        rows = pl.ds(pl.multiple_of(step * STEP, STEP), STEP)
        residue = plain[0][rows, :]
        if minus:
            residue = residue - plain[1][rows, :]
        high, low = halves(residue.T)
        both = jnp.concatenate([high, low], axis=0)
        piece(spans, step, diag_ref, buffer_ref, sems).wait()
        for a in range(spans):
            diag_high, diag_low = halves(buffer_ref[a, rows, :])
            one = mm(both, diag_high)
            total_ref[a] += one[:N] + one[N:] + mm(high, diag_low)

    if level == 0:
        out_refs[0][...] = total_ref[0].T
        return
    sub = sub_ref[0] % spans
    pieces = jnp.concatenate([total_ref[a] for a in range(spans)], axis=1)
    high, low = halves(pieces)
    both = jnp.concatenate([high, low], axis=0)
    for m in range(spans):
        picked = mm(both, hits(seen_ref, m, SLOTS_OF[level], spans))
        picked = (picked[:N] + picked[N:]).T
        own = total_ref[m ^ sub].T
        soon_ref, later_ref = out_refs[2 * m], out_refs[2 * m + 1]
        if level == 2:
            soon_ref[...] = picked[K:]
            later_ref[:K, :] = picked[:K]
            later_ref[K:, :] = own
        else:
            soon_ref[...] = picked
            later_ref[...] = own


def call(kernel, level, heights, scratch, plain, sub, *arrays):
    spans = 2**level
    vmem = pl.BlockSpec(memory_space=pltpu.VMEM)
    limit = FIRST_LIMIT if len(arrays) == 2 else VMEM_LIMIT
    specs = [vmem] * len(arrays)
    for place in [*plain, len(arrays) - 1]:
        specs[place] = pl.BlockSpec(memory_space=pltpu.HBM)
    return pl.pallas_call(
        functools.partial(kernel, level),
        in_specs=[pl.BlockSpec(memory_space=pltpu.SMEM)] + specs,
        out_specs=[vmem] * len(heights),
        scratch_shapes=[
            scratch,
            pltpu.VMEM((spans, R, C), jnp.float32),
            pltpu.SemaphoreType.DMA((R // STEP + len(plain),)),
        ]
        + [pltpu.VMEM((rows, N), jnp.float32) for rows in plain.values()],
        out_shape=[jax.ShapeDtypeStruct((h, N), jnp.float32) for h in heights],
        compiler_params=pltpu.CompilerParams(vmem_limit_bytes=limit),
        cost_estimate=pl.CostEstimate(
            flops=6 * R * spans * C * N, bytes_accessed=4 * R * spans * C, transcendentals=0
        ),
        name=f"{kernel.__name__}{level}",
    )(sub, *arrays)


def forward(level, sub, seen, updates, diag):
    scratch = pltpu.VMEM((2**level, C, 2 * N), jnp.bfloat16)
    plain = {} if level else {0: C}
    return call(forward_kernel, level, [R], scratch, plain, sub, seen, *updates, diag)[0]


def backward(level, sub, seen, residue, diag):
    heights = {0: [C], 1: [K, C] * 2, 2: [K, K + C] * 4}[level]
    scratch = pltpu.VMEM((2**level, N, C), jnp.float32)
    plain = {1 + place: R for place in range(len(residue))}
    return call(backward_kernel, level, heights, scratch, plain, sub, seen, *residue, diag)


def correct_kernel(slots, *refs):
    picked_refs, factor_ref, out_ref = refs[:-2], refs[-2], refs[-1]
    own, core, chip, both = (ref[...] for ref in picked_refs)
    total = (own + core) + (chip + both)
    pairs = [halves(total[i * K : (i + 1) * K]) for i in range(len(slots))]

    @pl.loop(0, R // STEP)
    def _(step):
        cols = pl.ds(pl.multiple_of(step * STEP, STEP), STEP)
        total = None
        for slot, (picked_high, picked_low) in zip(slots, pairs):
            high, low = halves(factor_ref[slot, :, cols].T)
            wide = mm(high, jnp.concatenate([picked_high, picked_low], axis=1))
            term = wide[:, :N] + wide[:, N:] + mm(low, picked_high)
            total = term if total is None else total + term
        out_ref[cols, :] = total


def correct(slots, picked, factor):
    vmem = pl.BlockSpec(memory_space=pltpu.VMEM)
    return pl.pallas_call(
        functools.partial(correct_kernel, slots),
        in_specs=[vmem] * (len(picked) + 1),
        out_specs=vmem,
        out_shape=jax.ShapeDtypeStruct((R, N), jnp.float32),
        compiler_params=pltpu.CompilerParams(vmem_limit_bytes=8 * 2**20),
        cost_estimate=pl.CostEstimate(
            flops=6 * R * K * N * len(slots), bytes_accessed=4 * R * K, transcendentals=0
        ),
        name=f"correct{len(slots)}",
    )(*picked, factor)


def swapped(value, axis, mask):
    pairs = [(source, source ^ mask) for source in range(lax.axis_size(axis))]
    return lax.ppermute(value, axis, pairs)


def fold_kernel(parts_ref, out_ref):
    total = parts_ref[0]
    for place in range(1, parts_ref.shape[0]):
        total = total + parts_ref[place]
    for place in range(parts_ref.shape[0]):
        out_ref[place] = total


def fold(parts):
    vmem = pl.BlockSpec(memory_space=pltpu.VMEM)
    return pl.pallas_call(
        fold_kernel,
        in_specs=[vmem],
        out_specs=vmem,
        out_shape=jax.ShapeDtypeStruct(parts.shape, jnp.float32),
        compiler_params=pltpu.CompilerParams(vmem_limit_bytes=4 * 2**20),
        name="fold",
    )(parts)


def col_sum(part, *held):
    blocks = part.reshape(lax.axis_size("col"), -1, N)
    own, *held = lax.optimization_barrier((fold(lax.all_to_all(blocks, "col", 0, 0)), *held))
    full = lax.all_to_all(own, "col", 0, 0).reshape(part.shape)
    return (full, *held)


def row_parts(part):
    return [part] + [swapped(part, "row", m) for m in (1, 2, 3)]


def row_sum(part):
    own, core, chip, both = row_parts(part)
    return (own + core) + (chip + both)


def sub_parts(part):
    return [part] + [swapped(part, "sub", m) for m in (1, 2, 3)]


def sub_sum(parts):
    return parts[0] + sum(swapped(parts[m], "sub", m) for m in range(1, len(parts)))


def on_device(pressure_rhs, diag_inverse, factor_blocks, row_lists):
    sub = lax.axis_index("sub").astype(jnp.int32).reshape(1)
    rhs = pressure_rhs[:, 0]
    diag = diag_inverse[0].transpose(1, 0, 2)
    factor = factor_blocks[:, 0]
    lists = row_lists[:, 0]
    targets = lists // S * C + lists % S - lax.axis_index("col") * C

    packed = jnp.concatenate(
        [
            rhs[1:].reshape(-1, N),
            targets.astype(jnp.float32),
            jnp.zeros((PACKED - LIST_AT - 3, N), jnp.float32),
        ]
    )
    def update(slot, solved):
        return jnp.dot(factor[slot], solved, precision=mode)

    y0, packed = col_sum(forward(0, sub, rhs, [], diag), packed)
    seen = jnp.stack(sub_parts(packed))
    u01 = row_sum(update(0, y0))
    part1 = forward(1, sub, seen, [u01, swapped(u01, "sub", 1)], diag)
    part1, u02 = lax.optimization_barrier((part1, update(1, y0)))
    y1, u02 = col_sum(part1, row_sum(u02))
    y1, u02 = lax.optimization_barrier((y1, jnp.concatenate(sub_parts(u02))))
    u12 = sub_parts(row_sum(update(2, y1)))
    (y2,) = col_sum(forward(2, sub, seen, [u02] + u12, diag))

    out2 = backward(2, sub, seen, [y2], diag)
    pick12 = row_parts(sub_sum(out2[0::2]))
    part1, *later = lax.optimization_barrier([correct((2,), pick12, factor)] + list(out2[1::2]))
    later = sub_sum(later)
    out1 = backward(1, sub, seen, [y1, *col_sum(part1)], diag)
    picked = row_parts(jnp.concatenate([sub_sum(out1[0::2]), later[:K]]))
    part0, x2 = lax.optimization_barrier((correct((0, 1), picked, factor), later[K:]))
    part0, x2, *later = col_sum(part0, x2, *out1[1::2])
    x2 = row_sum(x2)
    x1 = row_sum(sub_sum(later))
    (x0,) = backward(0, sub, rhs, [y0, part0], diag)
    x0 = row_sum(x0)
    return jnp.stack([x0, x1, x2])[:, None]


def solution(mesh):
    in_specs = (
        P(None, "sub", "col", None),
        P("sub", "row", None, "col"),
        P(None, "sub", "col", "row"),
        P(None, "sub", "col"),
    )
    out_specs = P(None, "sub", "col", None)
    return jax.shard_map(
        on_device, mesh=mesh, in_specs=in_specs, out_specs=out_specs, check_vma=False
    )
```

```python
import functools

import jax
import jax.numpy as jnp
from jax import lax
from jax.experimental import pallas as pl
from jax.experimental.pallas import tpu as pltpu
from jax.sharding import PartitionSpec as P

S = 4096
N = 128
C = 256
R = 1024
K = 128
STEP = 256
LEVELS = 3
VMEM_LIMIT = 46 * 2**20
FIRST_LIMIT = 58 * 2**20
LIST_AT = 2 * C
PACKED = 2 * C + 8
mode = lax.Precision.HIGH


def halves(value):
    high = value.astype(jnp.bfloat16)
    low = (value - high.astype(jnp.float32)).astype(jnp.bfloat16)
    return high, low


def mm(a, b):
    return jnp.dot(a, b, preferred_element_type=jnp.float32)


def hits(seen_ref, place, slots, panels):
    targets = jnp.concatenate(
        [seen_ref[place, LIST_AT + t : LIST_AT + t + 1, :] for t in slots], axis=1
    ).astype(jnp.int32)
    shape = (panels * C, K * len(slots))
    rows = lax.broadcasted_iota(jnp.int32, shape, 0)
    return jnp.where(rows == targets, 1.0, 0.0).astype(jnp.bfloat16)


SLOTS_OF = {1: (0,), 2: (1, 2)}


def piece(spans, step, diag_ref, buffer_ref, sems):
    rows = pl.ds(pl.multiple_of(step * STEP, STEP), STEP)
    source = diag_ref.at[pl.ds(spans - 1, spans), rows, :]
    return pltpu.make_async_copy(source, buffer_ref.at[:, rows, :], sems.at[step])


def fetch(*refs):
    for step in range(R // STEP):
        piece(refs[0], step, *refs[1:]).start()


def forward_kernel(level, sub_ref, seen_ref, *refs):
    spans = 2**level
    if level:
        update_refs, (diag_ref, out_ref, right_ref, buffer_ref, sems) = refs[:-5], refs[-5:]
    else:
        diag_ref, out_ref, right_ref, buffer_ref, sems, plain_ref = refs
        first = pltpu.make_async_copy(seen_ref.at[0], plain_ref, sems.at[R // STEP])
        first.start()
    fetch(spans, diag_ref, buffer_ref, sems)
    if level == 0:
        first.wait()
        high, low = halves(plain_ref[...])
        right_ref[0] = jnp.concatenate([high, low], axis=1)
    else:
        sub = sub_ref[0] % spans
        total = None
        for m in range(spans):
            if level == 1:
                own = update_refs[m][...]
            else:
                early = update_refs[0][m * K : (m + 1) * K, :]
                own = jnp.concatenate([early, update_refs[m + 1][...]], axis=0)
            high, low = halves(own)
            pair = jnp.concatenate([high, low], axis=1)
            term = mm(hits(seen_ref, m, SLOTS_OF[level], spans), pair)
            total = term if total is None else total + term
        total = total[:, :N] + total[:, N:]
        for a in range(spans):
            rhs = seen_ref[a ^ sub, (level - 1) * C : level * C, :]
            high, low = halves(rhs - total[a * C : (a + 1) * C])
            right_ref[a] = jnp.concatenate([high, low], axis=1)

    @pl.loop(0, R // STEP)
    def _(step):
        piece(spans, step, diag_ref, buffer_ref, sems).wait()
        rows = pl.ds(pl.multiple_of(step * STEP, STEP), STEP)
        wide, thin = None, None
        for a in range(spans):
            high, low = halves(buffer_ref[a, rows, :])
            one, two = mm(high, right_ref[a]), mm(low, right_ref[a, :, :N])
            wide = one if wide is None else wide + one
            thin = two if thin is None else thin + two
        out_ref[rows, :] = wide[:, :N] + wide[:, N:] + thin


def backward_kernel(level, sub_ref, seen_ref, base_ref, *refs):
    spans = 2**level
    minus = level < LEVELS - 1
    count = 2 if minus else 1
    plain, refs = refs[-count:], refs[:-count]
    total_ref, buffer_ref, sems = refs[-3:]
    diag_ref, out_refs = refs[count - 1], refs[count:-3]
    pairs = list(zip([base_ref, refs[0]], plain))
    copies = [
        pltpu.make_async_copy(source, target, sems.at[R // STEP + i])
        for i, (source, target) in enumerate(pairs)
    ]
    for copy in copies:
        copy.start()
    fetch(spans, diag_ref, buffer_ref, sems)
    total_ref[...] = jnp.zeros_like(total_ref)
    for copy in copies:
        copy.wait()

    @pl.loop(0, R // STEP)
    def _(step):
        rows = pl.ds(pl.multiple_of(step * STEP, STEP), STEP)
        residue = plain[0][rows, :]
        if minus:
            residue = residue - plain[1][rows, :]
        high, low = halves(residue.T)
        both = jnp.concatenate([high, low], axis=0)
        piece(spans, step, diag_ref, buffer_ref, sems).wait()
        for a in range(spans):
            diag_high, diag_low = halves(buffer_ref[a, rows, :])
            one = mm(both, diag_high)
            total_ref[a] += one[:N] + one[N:] + mm(high, diag_low)

    if level == 0:
        out_refs[0][...] = total_ref[0].T
        return
    sub = sub_ref[0] % spans
    pieces_ref = plain[0]
    for a in range(spans):
        pieces_ref[a * C : (a + 1) * C, :] = total_ref[a].T
    high, low = halves(pieces_ref[: spans * C, :])
    both = jnp.concatenate([high, low], axis=1)
    columns = lax.broadcasted_iota(jnp.int32, (K, spans * C), 1)
    for m in range(spans):
        lists = seen_ref[m, LIST_AT : LIST_AT + 8, :].T.astype(jnp.int32)
        picked = []
        for t in SLOTS_OF[level]:
            chosen = jnp.where(columns == lists[:, t : t + 1], 1.0, 0.0).astype(jnp.bfloat16)
            wide = mm(chosen, both)
            picked.append(wide[:, :N] + wide[:, N:])
        own = pieces_ref[pl.ds(pl.multiple_of((m ^ sub) * C, C), C), :]
        soon_ref, later_ref = out_refs[2 * m], out_refs[2 * m + 1]
        if level == 2:
            soon_ref[...] = picked[1]
            later_ref[:K, :] = picked[0]
            later_ref[K:, :] = own
        else:
            soon_ref[...] = picked[0]
            later_ref[...] = own


def call(kernel, level, heights, scratch, plain, sub, *arrays):
    spans = 2**level
    vmem = pl.BlockSpec(memory_space=pltpu.VMEM)
    limit = FIRST_LIMIT if len(arrays) == 2 else VMEM_LIMIT
    specs = [vmem] * len(arrays)
    for place in [*plain, len(arrays) - 1]:
        specs[place] = pl.BlockSpec(memory_space=pltpu.HBM)
    return pl.pallas_call(
        functools.partial(kernel, level),
        in_specs=[pl.BlockSpec(memory_space=pltpu.SMEM)] + specs,
        out_specs=[vmem] * len(heights),
        scratch_shapes=[
            scratch,
            pltpu.VMEM((spans, R, C), jnp.float32),
            pltpu.SemaphoreType.DMA((R // STEP + len(plain),)),
        ]
        + [pltpu.VMEM((rows, N), jnp.float32) for rows in plain.values()],
        out_shape=[jax.ShapeDtypeStruct((h, N), jnp.float32) for h in heights],
        compiler_params=pltpu.CompilerParams(vmem_limit_bytes=limit),
        cost_estimate=pl.CostEstimate(
            flops=6 * R * spans * C * N, bytes_accessed=4 * R * spans * C, transcendentals=0
        ),
        name=f"{kernel.__name__}{level}",
    )(sub, *arrays)


def forward(level, sub, seen, updates, diag):
    scratch = pltpu.VMEM((2**level, C, 2 * N), jnp.bfloat16)
    plain = {} if level else {0: C}
    return call(forward_kernel, level, [R], scratch, plain, sub, seen, *updates, diag)[0]


def backward(level, sub, seen, residue, diag):
    heights = {0: [C], 1: [K, C] * 2, 2: [K, K + C] * 4}[level]
    scratch = pltpu.VMEM((2**level, N, C), jnp.float32)
    plain = {1 + place: R for place in range(len(residue))}
    return call(backward_kernel, level, heights, scratch, plain, sub, seen, *residue, diag)


def correct_kernel(slots, *refs):
    picked_refs, factor_ref, out_ref = refs[:-2], refs[-2], refs[-1]
    own, core, chip, both = (ref[...] for ref in picked_refs)
    total = (own + core) + (chip + both)
    pairs = [halves(total[i * K : (i + 1) * K]) for i in range(len(slots))]

    @pl.loop(0, R // STEP)
    def _(step):
        cols = pl.ds(pl.multiple_of(step * STEP, STEP), STEP)
        total = None
        for slot, (picked_high, picked_low) in zip(slots, pairs):
            high, low = halves(factor_ref[slot, :, cols].T)
            wide = mm(high, jnp.concatenate([picked_high, picked_low], axis=1))
            term = wide[:, :N] + wide[:, N:] + mm(low, picked_high)
            total = term if total is None else total + term
        out_ref[cols, :] = total


def correct(slots, picked, factor):
    vmem = pl.BlockSpec(memory_space=pltpu.VMEM)
    return pl.pallas_call(
        functools.partial(correct_kernel, slots),
        in_specs=[vmem] * (len(picked) + 1),
        out_specs=vmem,
        out_shape=jax.ShapeDtypeStruct((R, N), jnp.float32),
        compiler_params=pltpu.CompilerParams(vmem_limit_bytes=8 * 2**20),
        cost_estimate=pl.CostEstimate(
            flops=6 * R * K * N * len(slots), bytes_accessed=4 * R * K, transcendentals=0
        ),
        name=f"correct{len(slots)}",
    )(*picked, factor)


def swapped(value, axis, mask):
    pairs = [(source, source ^ mask) for source in range(lax.axis_size(axis))]
    return lax.ppermute(value, axis, pairs)


def fold_kernel(parts_ref, out_ref):
    total = parts_ref[0]
    for place in range(1, parts_ref.shape[0]):
        total = total + parts_ref[place]
    for place in range(parts_ref.shape[0]):
        out_ref[place] = total


def fold(parts):
    vmem = pl.BlockSpec(memory_space=pltpu.VMEM)
    return pl.pallas_call(
        fold_kernel,
        in_specs=[vmem],
        out_specs=vmem,
        out_shape=jax.ShapeDtypeStruct(parts.shape, jnp.float32),
        compiler_params=pltpu.CompilerParams(vmem_limit_bytes=4 * 2**20),
        name="fold",
    )(parts)


def col_sum(part, *held):
    blocks = part.reshape(lax.axis_size("col"), -1, N)
    own, *held = lax.optimization_barrier((fold(lax.all_to_all(blocks, "col", 0, 0)), *held))
    full = lax.all_to_all(own, "col", 0, 0).reshape(part.shape)
    return (full, *held)


def row_parts(part):
    return [part] + [swapped(part, "row", m) for m in (1, 2, 3)]


def row_sum(part):
    own, core, chip, both = row_parts(part)
    return (own + core) + (chip + both)


def sub_parts(part):
    return [part] + [swapped(part, "sub", m) for m in (1, 2, 3)]


def sub_sum(parts):
    return parts[0] + sum(swapped(parts[m], "sub", m) for m in range(1, len(parts)))


def on_device(pressure_rhs, diag_inverse, factor_blocks, row_lists):
    sub = lax.axis_index("sub").astype(jnp.int32).reshape(1)
    rhs = pressure_rhs[:, 0]
    diag = diag_inverse[0].transpose(1, 0, 2)
    factor = factor_blocks[:, 0]
    lists = row_lists[:, 0]
    targets = lists // S * C + lists % S - lax.axis_index("col") * C

    packed = jnp.concatenate(
        [
            rhs[1:].reshape(-1, N),
            targets.astype(jnp.float32),
            jnp.zeros((PACKED - LIST_AT - 3, N), jnp.float32),
        ]
    )
    def update(slot, solved):
        return jnp.dot(factor[slot], solved, precision=mode)

    y0, packed = col_sum(forward(0, sub, rhs, [], diag), packed)
    seen = jnp.stack(sub_parts(packed))
    u01 = row_sum(update(0, y0))
    part1 = forward(1, sub, seen, [u01, swapped(u01, "sub", 1)], diag)
    part1, u02 = lax.optimization_barrier((part1, update(1, y0)))
    y1, u02 = col_sum(part1, row_sum(u02))
    y1, u02 = lax.optimization_barrier((y1, jnp.concatenate(sub_parts(u02))))
    u12 = sub_parts(row_sum(update(2, y1)))
    (y2,) = col_sum(forward(2, sub, seen, [u02] + u12, diag))

    out2 = backward(2, sub, seen, [y2], diag)
    pick12 = row_parts(sub_sum(out2[0::2]))
    part1, *later = lax.optimization_barrier([correct((2,), pick12, factor)] + list(out2[1::2]))
    later = sub_sum(later)
    out1 = backward(1, sub, seen, [y1, *col_sum(part1)], diag)
    picked = row_parts(jnp.concatenate([sub_sum(out1[0::2]), later[:K]]))
    part0, x2 = lax.optimization_barrier((correct((0, 1), picked, factor), later[K:]))
    part0, x2, *later = col_sum(part0, x2, *out1[1::2])
    x2 = row_sum(x2)
    x1 = row_sum(sub_sum(later))
    (x0,) = backward(0, sub, rhs, [y0, part0], diag)
    x0 = row_sum(x0)
    return jnp.stack([x0, x1, x2])[:, None]


def solution(mesh):
    in_specs = (
        P(None, "sub", "col", None),
        P("sub", "row", None, "col"),
        P(None, "sub", "col", "row"),
        P(None, "sub", "col"),
    )
    out_specs = P(None, "sub", "col", None)
    return jax.shard_map(
        on_device, mesh=mesh, in_specs=in_specs, out_specs=out_specs, check_vma=False
    )
```

```python
import functools

import jax
import jax.numpy as jnp
from jax import lax
from jax.experimental import pallas as pl
from jax.experimental.pallas import tpu as pltpu
from jax.sharding import PartitionSpec as P

S = 4096
N = 128
C = 256
R = 1024
K = 128
STEP = 256
LEVELS = 3
VMEM_LIMIT = 46 * 2**20
FIRST_LIMIT = 58 * 2**20
LIST_AT = 2 * C
PACKED = 2 * C + 8
mode = lax.Precision.HIGH


def halves(value):
    high = value.astype(jnp.bfloat16)
    low = (value - high.astype(jnp.float32)).astype(jnp.bfloat16)
    return high, low


def mm(a, b):
    return jnp.dot(a, b, preferred_element_type=jnp.float32)


def hits(seen_ref, lists, panels):
    targets = jnp.concatenate(
        [seen_ref[m, LIST_AT + t : LIST_AT + t + 1, :] for m, t in lists], axis=1
    ).astype(jnp.int32)
    shape = (panels * C, K * len(lists))
    rows = lax.broadcasted_iota(jnp.int32, shape, 0)
    return jnp.where(rows == targets, 1.0, 0.0).astype(jnp.bfloat16)


SLOTS_OF = {1: (0,), 2: (1, 2)}


def piece(spans, step, diag_ref, buffer_ref, sems):
    rows = pl.ds(pl.multiple_of(step * STEP, STEP), STEP)
    source = diag_ref.at[pl.ds(spans - 1, spans), rows, :]
    return pltpu.make_async_copy(source, buffer_ref.at[:, rows, :], sems.at[step])


def fetch(*refs):
    for step in range(R // STEP):
        piece(refs[0], step, *refs[1:]).start()


def forward_kernel(level, sub_ref, seen_ref, *refs):
    spans = 2**level
    if level:
        update_refs, (diag_ref, out_ref, right_ref, buffer_ref, sems) = refs[:-5], refs[-5:]
    else:
        diag_ref, out_ref, right_ref, buffer_ref, sems, plain_ref = refs
        first = pltpu.make_async_copy(seen_ref.at[0], plain_ref, sems.at[R // STEP])
        first.start()
    fetch(spans, diag_ref, buffer_ref, sems)
    if level == 0:
        first.wait()
        high, low = halves(plain_ref[...])
        right_ref[0] = jnp.concatenate([high, low], axis=1)
    else:
        sub = sub_ref[0] % spans
        total = None
        for m in range(spans):
            if level == 1:
                own = update_refs[m][...]
            else:
                early = update_refs[0][m * K : (m + 1) * K, :]
                own = jnp.concatenate([early, update_refs[m + 1][...]], axis=0)
            high, low = halves(own)
            pair = jnp.concatenate([high, low], axis=1)
            term = mm(hits(seen_ref, [(m, t) for t in SLOTS_OF[level]], spans), pair)
            total = term if total is None else total + term
        total = total[:, :N] + total[:, N:]
        for a in range(spans):
            rhs = seen_ref[a ^ sub, (level - 1) * C : level * C, :]
            high, low = halves(rhs - total[a * C : (a + 1) * C])
            right_ref[a] = jnp.concatenate([high, low], axis=1)

    @pl.loop(0, R // STEP)
    def _(step):
        piece(spans, step, diag_ref, buffer_ref, sems).wait()
        rows = pl.ds(pl.multiple_of(step * STEP, STEP), STEP)
        wide, thin = None, None
        for a in range(spans):
            high, low = halves(buffer_ref[a, rows, :])
            one, two = mm(high, right_ref[a]), mm(low, right_ref[a, :, :N])
            wide = one if wide is None else wide + one
            thin = two if thin is None else thin + two
        out_ref[rows, :] = wide[:, :N] + wide[:, N:] + thin


def backward_kernel(level, sub_ref, seen_ref, base_ref, *refs):
    spans = 2**level
    minus = level < LEVELS - 1
    count = 2 if minus else 1
    plain, refs = refs[-count:], refs[:-count]
    total_ref, buffer_ref, sems = refs[-3:]
    diag_ref, out_refs = refs[count - 1], refs[count:-3]
    pairs = list(zip([base_ref, refs[0]], plain))
    copies = [
        pltpu.make_async_copy(source, target, sems.at[R // STEP + i])
        for i, (source, target) in enumerate(pairs)
    ]
    for copy in copies:
        copy.start()
    fetch(spans, diag_ref, buffer_ref, sems)
    total_ref[...] = jnp.zeros_like(total_ref)
    for copy in copies:
        copy.wait()

    @pl.loop(0, R // STEP)
    def _(step):
        rows = pl.ds(pl.multiple_of(step * STEP, STEP), STEP)
        residue = plain[0][rows, :]
        if minus:
            residue = residue - plain[1][rows, :]
        high, low = halves(residue.T)
        both = jnp.concatenate([high, low], axis=0)
        piece(spans, step, diag_ref, buffer_ref, sems).wait()
        for a in range(spans):
            diag_high, diag_low = halves(buffer_ref[a, rows, :])
            one = mm(both, diag_high)
            total_ref[a] += one[:N] + one[N:] + mm(high, diag_low)

    if level == 0:
        out_refs[0][...] = total_ref[0].T
        return
    picks(seen_ref, total_ref, spans, 0 if level == 1 else 2, out_refs)
    if level == 2:
        out_refs[spans][...] = total_ref[...]
        return
    sub = sub_ref[0] % spans
    for m in range(spans):
        out_refs[spans + m][...] = total_ref[m ^ sub].T


def picks(seen_ref, total_ref, spans, slot, out_refs):
    pieces = jnp.concatenate([total_ref[a] for a in range(spans)], axis=1)
    high, low = halves(pieces)
    both = jnp.concatenate([high, low], axis=0)
    for m in range(0, spans, 2):
        picked = mm(both, hits(seen_ref, [(m, slot), (m + 1, slot)], spans))
        picked = (picked[:N] + picked[N:]).T
        out_refs[m][:K, :] = picked[:K]
        out_refs[m + 1][:K, :] = picked[K:]


def rest_kernel(sub_ref, seen_ref, total_ref, *out_refs):
    spans = 2 ** (LEVELS - 1)
    picks(seen_ref, total_ref, spans, 1, out_refs)
    for m in range(spans):
        out_refs[m][K:, :] = total_ref[m ^ sub_ref[0]].T


def rest(sub, seen, total):
    vmem = pl.BlockSpec(memory_space=pltpu.VMEM)
    shape = jax.ShapeDtypeStruct((K + C, N), jnp.float32)
    return pl.pallas_call(
        rest_kernel,
        in_specs=[pl.BlockSpec(memory_space=pltpu.SMEM), vmem, vmem],
        out_specs=[vmem] * 4,
        out_shape=[shape] * 4,
        compiler_params=pltpu.CompilerParams(vmem_limit_bytes=16 * 2**20),
        name="rest",
    )(sub, seen, total)


def call(kernel, level, heights, scratch, plain, sub, *arrays):
    spans = 2**level
    vmem = pl.BlockSpec(memory_space=pltpu.VMEM)
    shapes = [(h, N) for h in heights]
    if len(heights) == 4 and level == 2:
        shapes.append((spans, N, C))
    limit = FIRST_LIMIT if len(arrays) == 2 else VMEM_LIMIT
    specs = [vmem] * len(arrays)
    for place in [*plain, len(arrays) - 1]:
        specs[place] = pl.BlockSpec(memory_space=pltpu.HBM)
    return pl.pallas_call(
        functools.partial(kernel, level),
        in_specs=[pl.BlockSpec(memory_space=pltpu.SMEM)] + specs,
        out_specs=[vmem] * len(shapes),
        scratch_shapes=[
            scratch,
            pltpu.VMEM((spans, R, C), jnp.float32),
            pltpu.SemaphoreType.DMA((R // STEP + len(plain),)),
        ]
        + [pltpu.VMEM((rows, N), jnp.float32) for rows in plain.values()],
        out_shape=[jax.ShapeDtypeStruct(shape, jnp.float32) for shape in shapes],
        compiler_params=pltpu.CompilerParams(vmem_limit_bytes=limit),
        cost_estimate=pl.CostEstimate(
            flops=6 * R * spans * C * N, bytes_accessed=4 * R * spans * C, transcendentals=0
        ),
        name=f"{kernel.__name__}{level}",
    )(sub, *arrays)


def forward(level, sub, seen, updates, diag):
    scratch = pltpu.VMEM((2**level, C, 2 * N), jnp.bfloat16)
    plain = {} if level else {0: C}
    return call(forward_kernel, level, [R], scratch, plain, sub, seen, *updates, diag)[0]


def backward(level, sub, seen, residue, diag):
    heights = {0: [C], 1: [K, K, C, C], 2: [K] * 4}[level]
    scratch = pltpu.VMEM((2**level, N, C), jnp.float32)
    plain = {1 + place: R for place in range(len(residue))}
    return call(backward_kernel, level, heights, scratch, plain, sub, seen, *residue, diag)


def correct_kernel(slots, *refs):
    picked_refs, factor_ref, out_ref = refs[:-2], refs[-2], refs[-1]
    own, core, chip, both = (ref[...] for ref in picked_refs)
    total = (own + core) + (chip + both)
    pairs = [halves(total[i * K : (i + 1) * K]) for i in range(len(slots))]

    @pl.loop(0, R // STEP)
    def _(step):
        cols = pl.ds(pl.multiple_of(step * STEP, STEP), STEP)
        total = None
        for slot, (picked_high, picked_low) in zip(slots, pairs):
            high, low = halves(factor_ref[slot, :, cols].T)
            wide = mm(high, jnp.concatenate([picked_high, picked_low], axis=1))
            term = wide[:, :N] + wide[:, N:] + mm(low, picked_high)
            total = term if total is None else total + term
        out_ref[cols, :] = total


def correct(slots, picked, factor):
    vmem = pl.BlockSpec(memory_space=pltpu.VMEM)
    return pl.pallas_call(
        functools.partial(correct_kernel, slots),
        in_specs=[vmem] * (len(picked) + 1),
        out_specs=vmem,
        out_shape=jax.ShapeDtypeStruct((R, N), jnp.float32),
        compiler_params=pltpu.CompilerParams(vmem_limit_bytes=8 * 2**20),
        cost_estimate=pl.CostEstimate(
            flops=6 * R * K * N * len(slots), bytes_accessed=4 * R * K, transcendentals=0
        ),
        name=f"correct{len(slots)}",
    )(*picked, factor)


def swapped(value, axis, mask):
    pairs = [(source, source ^ mask) for source in range(lax.axis_size(axis))]
    return lax.ppermute(value, axis, pairs)


def fold_kernel(parts_ref, out_ref):
    total = parts_ref[0]
    for place in range(1, parts_ref.shape[0]):
        total = total + parts_ref[place]
    for place in range(parts_ref.shape[0]):
        out_ref[place] = total


def fold(parts):
    vmem = pl.BlockSpec(memory_space=pltpu.VMEM)
    return pl.pallas_call(
        fold_kernel,
        in_specs=[vmem],
        out_specs=vmem,
        out_shape=jax.ShapeDtypeStruct(parts.shape, jnp.float32),
        compiler_params=pltpu.CompilerParams(vmem_limit_bytes=4 * 2**20),
        name="fold",
    )(parts)


def col_sum(part, *held):
    blocks = part.reshape(lax.axis_size("col"), -1, N)
    own, *held = lax.optimization_barrier((fold(lax.all_to_all(blocks, "col", 0, 0)), *held))
    full = lax.all_to_all(own, "col", 0, 0).reshape(part.shape)
    return (full, *held)


def row_parts(part):
    return [part] + [swapped(part, "row", m) for m in (1, 2, 3)]


def row_sum(part):
    own, core, chip, both = row_parts(part)
    return (own + core) + (chip + both)


def sub_parts(part):
    return [part] + [swapped(part, "sub", m) for m in (1, 2, 3)]


def sub_sum(parts):
    return parts[0] + sum(swapped(parts[m], "sub", m) for m in range(1, len(parts)))


def on_device(pressure_rhs, diag_inverse, factor_blocks, row_lists):
    sub = lax.axis_index("sub").astype(jnp.int32).reshape(1)
    rhs = pressure_rhs[:, 0]
    diag = diag_inverse[0].transpose(1, 0, 2)
    factor = factor_blocks[:, 0]
    lists = row_lists[:, 0]
    targets = lists // S * C + lists % S - lax.axis_index("col") * C

    packed = jnp.concatenate(
        [
            rhs[1:].reshape(-1, N),
            targets.astype(jnp.float32),
            jnp.zeros((PACKED - LIST_AT - 3, N), jnp.float32),
        ]
    )
    def update(slot, solved):
        return jnp.dot(factor[slot], solved, precision=mode)

    y0, packed = col_sum(forward(0, sub, rhs, [], diag), packed)
    seen = jnp.stack(sub_parts(packed))
    u01 = row_sum(update(0, y0))
    part1 = forward(1, sub, seen, [u01, swapped(u01, "sub", 1)], diag)
    part1, u02 = lax.optimization_barrier((part1, update(1, y0)))
    y1, u02 = col_sum(part1, row_sum(u02))
    y1, u02 = lax.optimization_barrier((y1, jnp.concatenate(sub_parts(u02))))
    u12 = sub_parts(row_sum(update(2, y1)))
    (y2,) = col_sum(forward(2, sub, seen, [u02] + u12, diag))

    *soon, total = backward(2, sub, seen, [y2], diag)
    part1, total = col_sum(correct((2,), row_parts(sub_sum(soon)), factor), total)
    later = sub_sum(rest(sub, seen, total))
    out1 = backward(1, sub, seen, [y1, part1], diag)
    picked = row_parts(jnp.concatenate([sub_sum(out1[:2]), later[:K]]))
    part0, x2 = lax.optimization_barrier((correct((0, 1), picked, factor), later[K:]))
    part0, x2, *later = col_sum(part0, x2, *out1[2:])
    x2 = row_sum(x2)
    x1 = row_sum(sub_sum(later))
    (x0,) = backward(0, sub, rhs, [y0, part0], diag)
    x0 = row_sum(x0)
    return jnp.stack([x0, x1, x2])[:, None]


def solution(mesh):
    in_specs = (
        P(None, "sub", "col", None),
        P("sub", "row", None, "col"),
        P(None, "sub", "col", "row"),
        P(None, "sub", "col"),
    )
    out_specs = P(None, "sub", "col", None)
    return jax.shard_map(
        on_device, mesh=mesh, in_specs=in_specs, out_specs=out_specs, check_vma=False
    )
```

```python
import functools

import jax
import jax.numpy as jnp
from jax import lax
from jax.experimental import pallas as pl
from jax.experimental.pallas import tpu as pltpu
from jax.sharding import PartitionSpec as P

S = 4096
N = 128
C = 256
R = 1024
K = 128
STEP = 256
LEVELS = 3
VMEM_LIMIT = 46 * 2**20
FIRST_LIMIT = 58 * 2**20
LIST_AT = 2 * C
PACKED = 2 * C + 8
mode = lax.Precision.HIGH


def halves(value):
    high = value.astype(jnp.bfloat16)
    low = (value - high.astype(jnp.float32)).astype(jnp.bfloat16)
    return high, low


def mm(a, b):
    return jnp.dot(a, b, preferred_element_type=jnp.float32)


def hits(seen_ref, lists, panels):
    targets = jnp.concatenate(
        [seen_ref[m, LIST_AT + t : LIST_AT + t + 1, :] for m, t in lists], axis=1
    ).astype(jnp.int32)
    shape = (panels * C, K * len(lists))
    rows = lax.broadcasted_iota(jnp.int32, shape, 0)
    return jnp.where(rows == targets, 1.0, 0.0).astype(jnp.bfloat16)


def piece(spans, step, diag_ref, buffer_ref, sems):
    rows = pl.ds(pl.multiple_of(step * STEP, STEP), STEP)
    source = diag_ref.at[pl.ds(spans - 1, spans), rows, :]
    return pltpu.make_async_copy(source, buffer_ref.at[:, rows, :], sems.at[step])


def fetch(*refs):
    for step in range(R // STEP):
        piece(refs[0], step, *refs[1:]).start()


def forward_kernel(level, sub_ref, seen_ref, *refs):
    spans = 2**level
    if level:
        update_refs, (diag_ref, out_ref, right_ref, buffer_ref, sems) = refs[:-5], refs[-5:]
    else:
        diag_ref, out_ref, right_ref, buffer_ref, sems, plain_ref = refs
        first = pltpu.make_async_copy(seen_ref.at[0], plain_ref, sems.at[R // STEP])
        first.start()
    fetch(spans, diag_ref, buffer_ref, sems)
    if level == 0:
        first.wait()
        high, low = halves(plain_ref[...])
        right_ref[0] = jnp.concatenate([high, low], axis=1)
    else:
        sub = sub_ref[0] % spans
        total = None
        for m in range(spans):
            place = m + level - 1
            high, low = halves(update_refs[place][...])
            pair = jnp.concatenate([high, low], axis=1)
            term = mm(hits(seen_ref, [(m, 2 * level - 2)], spans), pair)
            total = term if total is None else total + term
        total = total[:, :N] + total[:, N:]
        for a in range(spans):
            rhs = seen_ref[a ^ sub, :C, :] if level == 1 else update_refs[0][a]
            high, low = halves(rhs - total[a * C : (a + 1) * C])
            right_ref[a] = jnp.concatenate([high, low], axis=1)

    @pl.loop(0, R // STEP)
    def _(step):
        piece(spans, step, diag_ref, buffer_ref, sems).wait()
        rows = pl.ds(pl.multiple_of(step * STEP, STEP), STEP)
        wide, thin = None, None
        for a in range(spans):
            high, low = halves(buffer_ref[a, rows, :])
            one, two = mm(high, right_ref[a]), mm(low, right_ref[a, :, :N])
            wide = one if wide is None else wide + one
            thin = two if thin is None else thin + two
        out_ref[rows, :] = wide[:, :N] + wide[:, N:] + thin


def backward_kernel(level, sub_ref, seen_ref, base_ref, *refs):
    spans = 2**level
    minus = level < LEVELS - 1
    count = 2 if minus else 1
    plain, refs = refs[-count:], refs[:-count]
    total_ref, buffer_ref, sems = refs[-3:]
    diag_ref, out_refs = refs[count - 1], refs[count:-3]
    pairs = list(zip([base_ref, refs[0]], plain))
    copies = [
        pltpu.make_async_copy(source, target, sems.at[R // STEP + i])
        for i, (source, target) in enumerate(pairs)
    ]
    for copy in copies:
        copy.start()
    fetch(spans, diag_ref, buffer_ref, sems)
    total_ref[...] = jnp.zeros_like(total_ref)
    for copy in copies:
        copy.wait()

    @pl.loop(0, R // STEP)
    def _(step):
        rows = pl.ds(pl.multiple_of(step * STEP, STEP), STEP)
        residue = plain[0][rows, :]
        if minus:
            residue = residue - plain[1][rows, :]
        high, low = halves(residue.T)
        both = jnp.concatenate([high, low], axis=0)
        piece(spans, step, diag_ref, buffer_ref, sems).wait()
        for a in range(spans):
            diag_high, diag_low = halves(buffer_ref[a, rows, :])
            one = mm(both, diag_high)
            total_ref[a] += one[:N] + one[N:] + mm(high, diag_low)

    if level == 0:
        out_refs[0][...] = total_ref[0].T
        return
    picks(seen_ref, total_ref, spans, 0 if level == 1 else 2, out_refs)
    if level == 2:
        out_refs[spans][...] = total_ref[...]
        return
    sub = sub_ref[0] % spans
    for m in range(spans):
        out_refs[spans + m][...] = total_ref[m ^ sub].T


def picks(seen_ref, total_ref, spans, slot, out_refs):
    pieces = jnp.concatenate([total_ref[a] for a in range(spans)], axis=1)
    high, low = halves(pieces)
    both = jnp.concatenate([high, low], axis=0)
    for m in range(0, spans, 2):
        picked = mm(both, hits(seen_ref, [(m, slot), (m + 1, slot)], spans))
        picked = (picked[:N] + picked[N:]).T
        out_refs[m][:K, :] = picked[:K]
        out_refs[m + 1][:K, :] = picked[K:]


def rest_kernel(sub_ref, seen_ref, total_ref, *out_refs):
    spans = 2 ** (LEVELS - 1)
    picks(seen_ref, total_ref, spans, 1, out_refs)
    for m in range(spans):
        out_refs[m][K:, :] = total_ref[m ^ sub_ref[0]].T


def early_kernel(sub_ref, seen_ref, update_ref, out_ref):
    spans = 2 ** (LEVELS - 1)
    total = None
    for m in range(0, spans, 2):
        high, low = halves(update_ref[m * K : (m + 2) * K, :])
        term = mm(hits(seen_ref, [(m, 1), (m + 1, 1)], spans), jnp.concatenate([high, low], axis=1))
        total = term if total is None else total + term
    total = total[:, :N] + total[:, N:]
    for a in range(spans):
        out_ref[a] = seen_ref[a ^ sub_ref[0], C : 2 * C, :] - total[a * C : (a + 1) * C]


def early(sub, seen, update):
    vmem = pl.BlockSpec(memory_space=pltpu.VMEM)
    return pl.pallas_call(
        early_kernel,
        in_specs=[pl.BlockSpec(memory_space=pltpu.SMEM), vmem, vmem],
        out_specs=vmem,
        out_shape=jax.ShapeDtypeStruct((4, C, N), jnp.float32),
        compiler_params=pltpu.CompilerParams(vmem_limit_bytes=16 * 2**20),
        name="early",
    )(sub, seen, update)


def rest(sub, seen, total):
    vmem = pl.BlockSpec(memory_space=pltpu.VMEM)
    shape = jax.ShapeDtypeStruct((K + C, N), jnp.float32)
    return pl.pallas_call(
        rest_kernel,
        in_specs=[pl.BlockSpec(memory_space=pltpu.SMEM), vmem, vmem],
        out_specs=[vmem] * 4,
        out_shape=[shape] * 4,
        compiler_params=pltpu.CompilerParams(vmem_limit_bytes=16 * 2**20),
        name="rest",
    )(sub, seen, total)


def call(kernel, level, heights, scratch, plain, sub, *arrays):
    spans = 2**level
    vmem = pl.BlockSpec(memory_space=pltpu.VMEM)
    shapes = [(h, N) for h in heights]
    if len(heights) == 4 and level == 2:
        shapes.append((spans, N, C))
    limit = FIRST_LIMIT if len(arrays) == 2 else VMEM_LIMIT
    specs = [vmem] * len(arrays)
    for place in [*plain, len(arrays) - 1]:
        specs[place] = pl.BlockSpec(memory_space=pltpu.HBM)
    return pl.pallas_call(
        functools.partial(kernel, level),
        in_specs=[pl.BlockSpec(memory_space=pltpu.SMEM)] + specs,
        out_specs=[vmem] * len(shapes),
        scratch_shapes=[
            scratch,
            pltpu.VMEM((spans, R, C), jnp.float32),
            pltpu.SemaphoreType.DMA((R // STEP + len(plain),)),
        ]
        + [pltpu.VMEM((rows, N), jnp.float32) for rows in plain.values()],
        out_shape=[jax.ShapeDtypeStruct(shape, jnp.float32) for shape in shapes],
        compiler_params=pltpu.CompilerParams(vmem_limit_bytes=limit),
        cost_estimate=pl.CostEstimate(
            flops=6 * R * spans * C * N, bytes_accessed=4 * R * spans * C, transcendentals=0
        ),
        name=f"{kernel.__name__}{level}",
    )(sub, *arrays)


def forward(level, sub, seen, updates, diag):
    scratch = pltpu.VMEM((2**level, C, 2 * N), jnp.bfloat16)
    plain = {} if level else {0: C}
    return call(forward_kernel, level, [R], scratch, plain, sub, seen, *updates, diag)[0]


def backward(level, sub, seen, residue, diag):
    heights = {0: [C], 1: [K, K, C, C], 2: [K] * 4}[level]
    scratch = pltpu.VMEM((2**level, N, C), jnp.float32)
    plain = {1 + place: R for place in range(len(residue))}
    return call(backward_kernel, level, heights, scratch, plain, sub, seen, *residue, diag)


def correct_kernel(slots, *refs):
    picked_refs, factor_ref, out_ref = refs[:-2], refs[-2], refs[-1]
    own, core, chip, both = (ref[...] for ref in picked_refs)
    total = (own + core) + (chip + both)
    pairs = [halves(total[i * K : (i + 1) * K]) for i in range(len(slots))]

    @pl.loop(0, R // STEP)
    def _(step):
        cols = pl.ds(pl.multiple_of(step * STEP, STEP), STEP)
        total = None
        for slot, (picked_high, picked_low) in zip(slots, pairs):
            high, low = halves(factor_ref[slot, :, cols].T)
            wide = mm(high, jnp.concatenate([picked_high, picked_low], axis=1))
            term = wide[:, :N] + wide[:, N:] + mm(low, picked_high)
            total = term if total is None else total + term
        out_ref[cols, :] = total


def correct(slots, picked, factor):
    vmem = pl.BlockSpec(memory_space=pltpu.VMEM)
    return pl.pallas_call(
        functools.partial(correct_kernel, slots),
        in_specs=[vmem] * (len(picked) + 1),
        out_specs=vmem,
        out_shape=jax.ShapeDtypeStruct((R, N), jnp.float32),
        compiler_params=pltpu.CompilerParams(vmem_limit_bytes=8 * 2**20),
        cost_estimate=pl.CostEstimate(
            flops=6 * R * K * N * len(slots), bytes_accessed=4 * R * K, transcendentals=0
        ),
        name=f"correct{len(slots)}",
    )(*picked, factor)


def swapped(value, axis, mask):
    pairs = [(source, source ^ mask) for source in range(lax.axis_size(axis))]
    return lax.ppermute(value, axis, pairs)


def fold_kernel(parts_ref, out_ref):
    total = parts_ref[0]
    for place in range(1, parts_ref.shape[0]):
        total = total + parts_ref[place]
    for place in range(parts_ref.shape[0]):
        out_ref[place] = total


def fold(parts):
    vmem = pl.BlockSpec(memory_space=pltpu.VMEM)
    return pl.pallas_call(
        fold_kernel,
        in_specs=[vmem],
        out_specs=vmem,
        out_shape=jax.ShapeDtypeStruct(parts.shape, jnp.float32),
        compiler_params=pltpu.CompilerParams(vmem_limit_bytes=4 * 2**20),
        name="fold",
    )(parts)


def col_sum(part, *held):
    blocks = part.reshape(lax.axis_size("col"), -1, N)
    own, *held = lax.optimization_barrier((fold(lax.all_to_all(blocks, "col", 0, 0)), *held))
    full = lax.all_to_all(own, "col", 0, 0).reshape(part.shape)
    return (full, *held)


def row_parts(part):
    return [part] + [swapped(part, "row", m) for m in (1, 2, 3)]


def row_sum(part):
    own, core, chip, both = row_parts(part)
    return (own + core) + (chip + both)


def sub_parts(part):
    return [part] + [swapped(part, "sub", m) for m in (1, 2, 3)]


def sub_sum(parts):
    return parts[0] + sum(swapped(parts[m], "sub", m) for m in range(1, len(parts)))


def on_device(pressure_rhs, diag_inverse, factor_blocks, row_lists):
    sub = lax.axis_index("sub").astype(jnp.int32).reshape(1)
    rhs = pressure_rhs[:, 0]
    diag = diag_inverse[0].transpose(1, 0, 2)
    factor = factor_blocks[:, 0]
    lists = row_lists[:, 0]
    targets = lists // S * C + lists % S - lax.axis_index("col") * C

    packed = jnp.concatenate(
        [
            rhs[1:].reshape(-1, N),
            targets.astype(jnp.float32),
            jnp.zeros((PACKED - LIST_AT - 3, N), jnp.float32),
        ]
    )
    def update(slot, solved):
        return jnp.dot(factor[slot], solved, precision=mode)

    y0, packed = col_sum(forward(0, sub, rhs, [], diag), packed)
    seen = jnp.stack(sub_parts(packed))
    u01 = row_sum(update(0, y0))
    part1 = forward(1, sub, seen, [u01, swapped(u01, "sub", 1)], diag)
    part1, u02 = lax.optimization_barrier((part1, update(1, y0)))
    y1, u02 = col_sum(part1, row_sum(u02))
    y1, u02 = lax.optimization_barrier((y1, early(sub, seen, jnp.concatenate(sub_parts(u02)))))
    u12 = sub_parts(row_sum(update(2, y1)))
    (y2,) = col_sum(forward(2, sub, seen, [u02] + u12, diag))

    *soon, total = backward(2, sub, seen, [y2], diag)
    part1, total = col_sum(correct((2,), row_parts(sub_sum(soon)), factor), total)
    later = sub_sum(rest(sub, seen, total))
    out1 = backward(1, sub, seen, [y1, part1], diag)
    picked = row_parts(jnp.concatenate([sub_sum(out1[:2]), later[:K]]))
    part0, x2 = lax.optimization_barrier((correct((0, 1), picked, factor), later[K:]))
    part0, x2, *later = col_sum(part0, x2, *out1[2:])
    x2 = row_sum(x2)
    x1 = row_sum(sub_sum(later))
    (x0,) = backward(0, sub, rhs, [y0, part0], diag)
    x0 = row_sum(x0)
    return jnp.stack([x0, x1, x2])[:, None]


def solution(mesh):
    in_specs = (
        P(None, "sub", "col", None),
        P("sub", "row", None, "col"),
        P(None, "sub", "col", "row"),
        P(None, "sub", "col"),
    )
    out_specs = P(None, "sub", "col", None)
    return jax.shard_map(
        on_device, mesh=mesh, in_specs=in_specs, out_specs=out_specs, check_vma=False
    )
```
